512 devices in a mesh: grp: 16 (over y, core), pts: 32 (over x, z).
Axes of the slice: x: 4, y: 8, z: 8, core: 2. Of those that a mesh axis runs over, the one named last changes fastest.
Arguments:
- embeddings: bfloat16 [262144, 768], P(('grp', 'pts')), may hold values from -16 to 16
- frequencies: bfloat16 [768, 256], replicated, may hold values from -6 to 6
- phases: float32 [9, 256], replicated, may hold values from -3.140625 to 3.140625
- solution: float32 [32, 262144], P(None, ('grp', 'pts')), may hold values from -6 to 6
- residual: float32 [32, 262144], P(None, ('grp', 'pts')), may hold values from -100 to 100
- direction: float32 [32, 262144], P(None, ('grp', 'pts')), may hold values from -100 to 100
Outputs:
- new_solution: float32 [32, 262144], P(None, ('grp', 'pts'))
- new_residual: float32 [32, 262144], P(None, ('grp', 'pts'))
- new_direction: float32 [32, 262144], P(None, ('grp', 'pts'))
The draws below stay inside these ranges and needn't reach their ends.
All inputs are finite; a program needn't handle non-finite values.
Results may differ from the reference program's by a relative error of at most 0.0003.
Values sent between devices are 32-bit elements; how exact they have to be, the bound alone decides.
No kernel may reach another device: no remote copies, remote signals or barrier semaphores. Data moves between devices by JAX's collectives and lax.ppermute only.
A program may use at most 64 MiB of HBM per device.

```python
import math
import jax
import jax.numpy as jnp
from jax import lax

E = 768
K = 256
R = 32
LEAF = 512
LEVELS = 9
POINTS = 262144
N_GRP = 16
N_PTS = 32


def scaled_field(key):
    first, second, third = jax.random.split(key, 3)
    devices = POINTS // LEAF
    owner = (jnp.arange(POINTS) // LEAF).astype(jnp.float32)
    rising = 1.0 + 2.0 * owner / max(devices - 1, 1)
    row_scale = rising * jnp.exp(jax.random.uniform(first, (POINTS,), jnp.float32, 0.0, math.log(4.0))) / 2.0
    column_scale = jnp.exp(jax.random.uniform(second, (R, 1), jnp.float32, math.log(0.3), math.log(3.0)))
    base = jnp.clip(jax.random.normal(third, (R, POINTS), jnp.float32), -5.0, 5.0)
    return (base * row_scale[None, :] * column_scale).astype(jnp.float32)


def draw_residual(key, part):
    return scaled_field(jax.random.fold_in(key, 101))


def draw_direction(key, part):
    return scaled_field(jax.random.fold_in(key, 202))


def draw_embeddings(key, part):
    key_centre, key_basis, key_coord, key_jitter = jax.random.split(jax.random.fold_in(key, 303), 4)
    leaves = POINTS // LEAF
    latent_dim = 16
    spread = 0.18
    centres = jnp.clip(jax.random.normal(key_centre, (leaves, 1, E), jnp.float32), -5.0, 5.0) / math.sqrt(E)
    latent_basis = jnp.clip(jax.random.normal(key_basis, (leaves, latent_dim, E), jnp.float32), -5.0, 5.0) / math.sqrt(E)
    coords = spread * jnp.clip(jax.random.normal(key_coord, (leaves, LEAF, latent_dim), jnp.float32), -5.0, 5.0)
    jitter_term = 0.3 * jnp.clip(jax.random.normal(key_jitter, (leaves, LEAF, E), jnp.float32), -5.0, 5.0) / math.sqrt(E)
    placed = jnp.einsum('bpl,ble->bpe', coords, latent_basis, precision=lax.Precision.HIGHEST)
    points = centres + placed + jitter_term
    return points.reshape(POINTS, E).astype(jnp.bfloat16)


def steps_of(stream_key, shape, cuts, smallest, largest):
    gain = 1.0
    for position, shards_of in cuts:
        draws = jax.random.uniform(jax.random.fold_in(jax.random.fold_in(stream_key, 6), position), (shards_of,), jnp.float32, smallest / len(cuts), largest / len(cuts))
        gain = gain * jnp.repeat(jnp.exp(draws), shape[position] // shards_of).reshape((-1,) + (1,) * (len(shape) - 1 - position))
    return gain


def centred(rng, shape, deviation, reach, shards=(), kind=jnp.bfloat16):
    drawn = deviation * jax.random.normal(rng, shape, jnp.float32)
    if shards:
        drawn = drawn * steps_of(rng, shape, shards, -0.22, 0.18)
    return jnp.clip(drawn, -reach, reach).astype(kind)


def setup_inputs(seed: int = 0) -> dict:
    key_list = jax.random.split(jax.random.key(seed), 7)
    embeddings = draw_embeddings(jax.random.fold_in(key_list[6], 71), 0)
    frequencies = centred(key_list[1], (E, K), 1.0, 6.0)
    phases = jnp.clip(jax.random.uniform(key_list[2], (LEVELS, K), jnp.float32, -3.140625, 3.140625), -3.140625, 3.140625)
    solution = centred(key_list[3], (R, POINTS), 1.0, 6.0, ((1, 512),), jnp.float32)
    residual = draw_residual(jax.random.fold_in(key_list[6], 71), 0)
    direction = draw_direction(jax.random.fold_in(key_list[6], 71), 0)
    return {"embeddings": embeddings, "frequencies": frequencies, "phases": phases, "solution": solution, "residual": residual, "direction": direction}


ridge_term = 0.5
highest = lax.Precision.HIGHEST

def leaf_kernel_block(leaf_points):
    squares = lax.optimization_barrier(jnp.sum(jnp.square(leaf_points.astype(jnp.float32)), axis=1))
    inner_products = jnp.dot(leaf_points.astype(jnp.float32), leaf_points.T.astype(jnp.float32), preferred_element_type=jnp.float32)
    distances = squares[:, None] + squares[None, :] - 2.0 * inner_products
    return math.sqrt(K / LEAF) * jnp.exp(-distances / 0.5)

def leaf_factor(kernel):
    identity = jnp.eye(LEAF, dtype=jnp.float32)
    return jnp.linalg.cholesky(kernel + ridge_term * identity)

def solve_rows(rows, factor):
    halfway = lax.linalg.triangular_solve(factor, rows, left_side=False, lower=True, transpose_a=True)
    return lax.linalg.triangular_solve(factor, halfway, left_side=False, lower=True)

def feature_panel(projected, phase_row, depth):
    length_scale = 0.5 * 2.0 ** (depth / 8.0)
    return math.sqrt(2.0 / K) * jnp.cos(projected / length_scale + phase_row)

def reference(embeddings, frequencies, phases, solution, residual, direction):
    devices = N_GRP * N_PTS
    total_points = devices * LEAF
    leaf_points = embeddings.reshape(devices, LEAF, E)

    def to_leaves(field):
        return field.reshape(R, devices, LEAF).transpose(1, 0, 2)

    def from_leaves(leaves):
        return leaves.transpose(1, 0, 2).reshape(R, total_points)

    def first_pass(triple):
        kernel = leaf_kernel_block(triple[0])
        factor = leaf_factor(kernel)
        return (jnp.dot(triple[1], kernel, precision=highest), solve_rows(triple[2], factor))
    near_terms, solved_leaves = lax.map(first_pass, (leaf_points, to_leaves(direction), to_leaves(residual)))
    preconditioned = from_leaves(solved_leaves)
    norm_old = lax.optimization_barrier(jnp.sum(residual * preconditioned, axis=1))
    operator_image = ridge_term * direction + from_leaves(near_terms)
    projected = jnp.dot(embeddings.astype(jnp.float32), frequencies.astype(jnp.float32), preferred_element_type=jnp.float32)
    for depth in range(1, LEVELS + 1):
        feature_block = feature_panel(projected, phases[depth - 1], depth)
        node_points = LEAF * 2 ** depth
        node_count = total_points // node_points
        node_blocks = feature_block.reshape(node_count, node_points, K)
        pieces = direction.reshape(R, node_count, node_points)
        totals = jnp.einsum('rns,nsk->rnk', pieces, node_blocks, precision=highest)
        spread = jnp.einsum('rnk,nsk->rns', totals, node_blocks, precision=highest)
        operator_image = operator_image + math.sqrt(K / node_points) * spread.reshape(R, total_points)
    curvature = lax.optimization_barrier(jnp.sum(direction * operator_image, axis=1))
    step_size = norm_old / curvature
    new_solution = solution + step_size[:, None] * direction
    new_residual = residual - step_size[:, None] * operator_image

    def second_pass(pair):
        return solve_rows(pair[1], leaf_factor(leaf_kernel_block(pair[0])))
    next_preconditioned = from_leaves(lax.map(second_pass, (leaf_points, to_leaves(new_residual))))
    norm_new = lax.optimization_barrier(jnp.sum(new_residual * next_preconditioned, axis=1))
    new_direction = next_preconditioned + (norm_new / norm_old)[:, None] * direction
    return (new_solution, new_residual, new_direction)
```

```python
import math

import jax
import jax.numpy as jnp
import numpy as np
from jax import lax
from jax.experimental import pallas as pl
from jax.experimental.pallas import tpu as pltpu
from jax.sharding import Mesh
from jax.sharding import PartitionSpec as P

AXES = ("y", "c", "x", "z")
LEAF, EMBED, RANK, ROWS, LEVELS = 512, 768, 256, 32, 9
PTS, GRP = 32, 16
RIDGE = 0.5
HALF = LEAF // 2
CHUNK = 32

f32 = jnp.float32
bf16 = jnp.bfloat16
highest = lax.Precision.HIGHEST


def cosine_coefficients():
    cheb = np.polynomial.chebyshev
    nodes = np.cos(np.pi * (np.arange(64) + 0.5) / 64)
    squares = np.pi**2 * (nodes + 1.0) / 2.0
    series = cheb.chebfit(nodes, np.cos(np.sqrt(squares)), 7)
    poly = np.polynomial.Polynomial(cheb.cheb2poly(series))
    shifted = poly(np.polynomial.Polynomial([-1.0, 2.0 / np.pi**2]))
    return [float(value) for value in shifted.coef * math.sqrt(2.0 / RANK)]


COSINE = cosine_coefficients()
TURN_HIGH = 6.28125
TURN_LOW = 2.0 * math.pi - TURN_HIGH


def scaled_cosine(angle):
    turns = jnp.round(angle * (1.0 / (2.0 * math.pi)))
    reduced = (angle - turns * TURN_HIGH) - turns * TURN_LOW
    square = reduced * reduced
    value = jnp.full_like(square, COSINE[-1])
    for coefficient in COSINE[-2::-1]:
        value = value * square + coefficient
    return value


def split(value):
    high = value.astype(bf16)
    return high, (value - high.astype(f32)).astype(bf16)


def mm(left, right):
    return jnp.dot(left, right, preferred_element_type=f32)


def mm_t(left, right, precision=None):
    return lax.dot_general(
        left, right, (((1,), (1,)), ((), ())), preferred_element_type=f32, precision=precision
    )


def mm3(left, right):
    return mm(left[0], right[0]) + (mm(left[0], right[1]) + mm(left[1], right[0]))


def mm6(left, right):
    return jnp.dot(left, right, preferred_element_type=f32, precision=highest)


def length_scale(depth):
    return 0.5 * 2.0 ** (depth / 8.0)


def features_kernel(emb, freq, phase, direction, feat, part_first, part, proj, high, low):
    proj[...] = mm(emb[...], freq[...])

    def chunk(step, carry):
        rows = pl.ds(pl.multiple_of(step * CHUNK, CHUNK), CHUNK)
        block = proj[rows, :]
        for level in range(LEVELS):
            angle = block * (1.0 / length_scale(level + 1)) + phase[level : level + 1, :]
            value = scaled_cosine(angle)
            feat[level, rows, :] = value
            high_part, low_part = split(value)
            high[level, rows, :] = high_part
            low[level, rows, :] = low_part
        return carry

    lax.fori_loop(0, LEAF // CHUNK, chunk, 0)
    direction_high, direction_low = split(direction[...])
    stacked = jnp.concatenate([direction_high, direction_low], axis=0)
    for level in range(LEVELS):
        both = mm(stacked, high[level])
        total = both[:ROWS] + (both[ROWS:] + mm(direction_high, low[level]))
        if level == 0:
            part_first[...] = total
        else:
            slot = 2 * (level - 1)
            part[pl.ds(slot, ROWS, stride=16), :] = total[:, :128]
            part[pl.ds(slot + 1, ROWS, stride=16), :] = total[:, 128:]


def eye_block():
    row = lax.broadcasted_iota(jnp.int32, (HALF, HALF), 0)
    column = lax.broadcasted_iota(jnp.int32, (HALF, HALF), 1)
    return jnp.where(row == column, 1.0, 0.0).astype(f32)


def inverse_block(block, largest):
    eye = eye_block()
    start = 2.0 / (RIDGE + largest)
    scale = jnp.minimum((largest + RIDGE) / jnp.maximum(largest - RIDGE, 1e-3), 1e4)
    error = eye - start * block
    inverse = None
    for step in range(6):
        double = 2.0 * scale * scale
        gain = double / (double - 1.0)
        error_parts = split(error)
        if step == 0:
            inverse = (gain * start) * (eye + error)
        else:
            inverse = gain * (inverse + mm3(split(inverse), error_parts))
        if step < 5:
            error = gain * mm3(error_parts, error_parts) - (gain / double) * eye
            scale = jnp.minimum(double - 1.0, 1e4)
    block_parts = split(block)
    for step in range(3):
        if step < 2:
            error = eye - mm3(block_parts, split(inverse))
        else:
            error = eye - mm6(block, inverse)
        inverse_high, inverse_low = split(inverse)
        if step < 1:
            inverse = inverse + mm3((inverse_high, inverse_low), split(error))
        else:
            inverse = inverse + mm(inverse_high, error.astype(bf16))
    return inverse


def leaf_kernel(emb, direction, residual, inv, solved, near, matrix):
    points = emb[...]
    wide = points.astype(f32)
    square_high, square_low = split(wide * wide)
    ones_left = jnp.ones((8, EMBED), bf16)
    ones_right = jnp.ones((EMBED, 128), bf16)
    along = (mm_t(ones_left, square_high) + mm_t(ones_left, square_low))[:1, :]
    down = (mm(square_high, ones_right) + mm(square_low, ones_right))[:, :1]
    inv[...] = down + along
    matrix[...] = mm_t(points, points)

    def chunk(step, carry):
        begin = pl.multiple_of(step * CHUNK, CHUNK)
        rows = pl.ds(begin, CHUNK)
        distances = inv[rows, :] - 2.0 * matrix[rows, :]
        value = math.sqrt(RANK / LEAF) * jnp.exp(distances * (-1.0 / 0.5))
        row = begin + lax.broadcasted_iota(jnp.int32, (CHUNK, LEAF), 0)
        column = lax.broadcasted_iota(jnp.int32, (CHUNK, LEAF), 1)
        matrix[rows, :] = value + jnp.where(row == column, RIDGE, 0.0)
        return carry

    lax.fori_loop(0, LEAF // CHUNK, chunk, 0)
    near[...] = mm6(direction[...], matrix[...])
    sums = jnp.sum(matrix[...], axis=0, keepdims=True)
    largest = jnp.max(sums, axis=1, keepdims=True)
    corner = matrix[:HALF, :HALF]
    side = matrix[:HALF, HALF:]
    first = inverse_block(corner, largest)
    across = mm6(first, side)
    across_t = jnp.transpose(across)
    schur = matrix[HALF:, HALF:] - mm6(across_t, side)
    second = inverse_block(schur, largest)
    lower = -mm6(second, across_t)
    inv[:HALF, :HALF] = first - mm6(across, lower)
    inv[HALF:, :HALF] = lower
    inv[:HALF, HALF:] = jnp.transpose(lower)
    inv[HALF:, HALF:] = second
    solved[...] = mm6(residual[...], inv[...])


def middle_send_kernel(received, out):
    total = received[0, 8:16, :]
    for source in range(1, PTS):
        total = total + received[source, 8:16, :]
    for target in range(GRP):
        out[target] = total


def row_select(tiles):
    row = lax.broadcasted_iota(jnp.int32, (8, 128), 0)
    return jnp.where(row < 2, tiles[0], jnp.where(row < 4, tiles[1], jnp.where(row < 6, tiles[2], tiles[3])))


def middle_return_kernel(place, received, wide, out):
    sums = [received[source, 0:8, :] for source in range(PTS)]
    stages = []
    for _ in range(5):
        sums = [sums[2 * n] + sums[2 * n + 1] for n in range(len(sums) // 2)]
        stages.append(sums)
    line = place[0]
    upper = []
    for depth in range(4):
        base = (line >> depth) << (depth + 1)
        total = wide[base] + wide[base + 1]
        for source in range(2, 2 ** (depth + 1)):
            total = total + wide[base + source]
        upper.append(total)
    top = row_select(upper)
    for node in range(8):
        low = row_select([stages[1][node], stages[2][node // 2], stages[3][node // 4], stages[4][0]])
        for leaf in range(4):
            out[node * 4 + leaf, 0:8, :] = low
            out[node * 4 + leaf, 8:16, :] = top


def image_kernel(
    own_first, other_first, returned, feat, near, direction, residual, solved, inv, image, shifted, out
):
    spread = near[...]
    for level in range(LEVELS):
        if level == 0:
            total = own_first[...] + other_first[...]
        else:
            slot = 2 * (level - 1)
            total = jnp.concatenate(
                [returned[pl.ds(slot, ROWS, stride=16), :], returned[pl.ds(slot + 1, ROWS, stride=16), :]],
                axis=1,
            )
        weight = math.sqrt(RANK / (LEAF * 2 ** (level + 1)))
        spread = spread + mm_t(total * weight, feat[level], highest)
    image[...] = spread
    moved = mm6(spread, inv[...])
    shifted[...] = moved
    residual_solved = solved[...]
    products = jnp.concatenate(
        [residual[...] * residual_solved, direction[...] * spread, residual_solved * spread, spread * moved], axis=0
    )
    sums = mm_t(jnp.ones((8, LEAF), f32), products, highest)
    out[...] = sums


def sum_spread_kernel(received, out):
    total = received[0]
    for source in range(1, PTS):
        total = total + received[source]
    for target in range(GRP):
        out[target] = total


def finish_kernel(received, solution, residual, direction, solved, image, shifted, new_solution, new_residual, new_direction):
    total = received[0]
    for source in range(1, GRP):
        total = total + received[source]
    row = lax.broadcasted_iota(jnp.int32, (ROWS, 128), 0)
    column = lax.broadcasted_iota(jnp.int32, (ROWS, 128), 1)
    spread = jnp.broadcast_to(total, (ROWS, 128))

    def pick(slot):
        return jnp.sum(jnp.where(column == row + ROWS * slot, spread, 0.0), axis=1, keepdims=True)

    norm_old, curvature, cross, moved = pick(0), pick(1), pick(2), pick(3)
    step = norm_old / curvature
    norm_new = norm_old - step * (2.0 * cross - step * moved)
    ratio = norm_new / norm_old
    direction_value = direction[...]
    new_solution[...] = solution[...] + step * direction_value
    new_residual[...] = residual[...] - step * image[...]
    new_direction[...] = (solved[...] - step * shifted[...]) + ratio * direction_value


def whole(shape, dtype=f32):
    return jax.ShapeDtypeStruct(shape, dtype)


def call(kernel, outs, *args, scratch=(), name=None, scalars=0):
    vmem = pl.BlockSpec(memory_space=pltpu.VMEM)
    smem = pl.BlockSpec(memory_space=pltpu.SMEM)
    single = not isinstance(outs, (tuple, list))
    return pl.pallas_call(
        kernel,
        out_shape=outs,
        in_specs=[smem if n < scalars else vmem for n in range(len(args))],
        out_specs=vmem if single else tuple(vmem for _ in outs),
        scratch_shapes=list(scratch),
        compiler_params=pltpu.CompilerParams(vmem_limit_bytes=50 * 2**20),
        name=name,
    )(*args)


def exchange(value, axes):
    return lax.all_to_all(value, axes, 0, 0, tiled=True)


def body(embeddings, frequencies, phases, solution, residual, direction):
    rows = whole((ROWS, LEAF))
    feat, part_first, part = call(
        features_kernel,
        (whole((LEVELS, LEAF, RANK)), whole((ROWS, RANK)), whole((ROWS * 16, 128))),
        embeddings, frequencies, phases, direction,
        scratch=(
            pltpu.VMEM((LEAF, RANK), f32),
            pltpu.VMEM((LEVELS, LEAF, RANK), bf16),
            pltpu.VMEM((LEVELS, LEAF, RANK), bf16),
        ),
        name="features",
    )
    other_first = lax.ppermute(part_first, "z", [(n, n ^ 1) for n in range(8)])
    received = exchange(part.reshape(ROWS, 16, 128), ("x", "z"))
    inv, solved, near = call(
        leaf_kernel, (whole((LEAF, LEAF)), rows, rows), embeddings, direction, residual,
        scratch=(pltpu.VMEM((LEAF, LEAF), f32),), name="leaf",
    )
    middle = call(middle_send_kernel, whole((GRP, 8, 128)), received, name="middle_send")
    wide = exchange(middle, ("y", "c"))
    place = lax.axis_index("y").astype(jnp.int32).reshape(1)
    back = call(middle_return_kernel, whole((PTS, 16, 128)), place, received, wide, name="middle_return", scalars=1)
    returned = exchange(back, ("x", "z"))
    image, shifted, sums = call(
        image_kernel, (rows, rows, whole((8, 128))),
        part_first, other_first, returned.reshape(PTS * 16, 128), feat, near, direction, residual, solved, inv,
        name="image",
    )
    gathered = exchange(jnp.broadcast_to(sums[None, :1, :], (PTS, 1, 128)), ("x", "z"))
    middle_sums = call(sum_spread_kernel, whole((GRP, 1, 128)), gathered, name="sum_spread")
    totals = exchange(middle_sums, ("y", "c"))
    return call(
        finish_kernel, (rows, rows, rows), totals, solution, residual, direction, solved, image, shifted, name="finish"
    )


def solution(mesh):
    torus = Mesh(mesh.devices.reshape(8, 2, 4, 8), AXES)
    columns = P(None, AXES)
    return jax.shard_map(
        body,
        mesh=torus,
        in_specs=(P(AXES, None), P(), P(), columns, columns, columns),
        out_specs=(columns, columns, columns),
        check_vma=False,
    )
```

```python
import math

import jax
import jax.numpy as jnp
import numpy as np
from jax import lax
from jax.experimental import pallas as pl
from jax.experimental.pallas import tpu as pltpu
from jax.sharding import Mesh
from jax.sharding import PartitionSpec as P

AXES = ("y", "c", "x", "z")
LEAF, EMBED, RANK, ROWS, LEVELS = 512, 768, 256, 32, 9
PTS, GRP = 32, 16
RIDGE = 0.5
HALF = LEAF // 2
CHUNK = 32

f32 = jnp.float32
bf16 = jnp.bfloat16
highest = lax.Precision.HIGHEST


def cosine_coefficients():
    cheb = np.polynomial.chebyshev
    nodes = np.cos(np.pi * (np.arange(64) + 0.5) / 64)
    squares = np.pi**2 * (nodes + 1.0) / 2.0
    series = cheb.chebfit(nodes, np.cos(np.sqrt(squares)), 7)
    poly = np.polynomial.Polynomial(cheb.cheb2poly(series))
    shifted = poly(np.polynomial.Polynomial([-1.0, 2.0 / np.pi**2]))
    return [float(value) for value in shifted.coef * math.sqrt(2.0 / RANK)]


COSINE = cosine_coefficients()
TURN_HIGH = 6.28125
TURN_LOW = 2.0 * math.pi - TURN_HIGH


def scaled_cosine(angle):
    turns = jnp.round(angle * (1.0 / (2.0 * math.pi)))
    reduced = (angle - turns * TURN_HIGH) - turns * TURN_LOW
    square = reduced * reduced
    value = jnp.full_like(square, COSINE[-1])
    for coefficient in COSINE[-2::-1]:
        value = value * square + coefficient
    return value


def split(value):
    high = value.astype(bf16)
    return high, (value - high.astype(f32)).astype(bf16)


def mm(left, right):
    return jnp.dot(left, right, preferred_element_type=f32)


def mm_t(left, right, precision=None):
    return lax.dot_general(
        left, right, (((1,), (1,)), ((), ())), preferred_element_type=f32, precision=precision
    )


def mm3(left, right):
    return mm(left[0], right[0]) + (mm(left[0], right[1]) + mm(left[1], right[0]))


def planes(value):
    high = value.astype(bf16)
    rest = value - high.astype(f32)
    middle = rest.astype(bf16)
    return high, middle, (rest - middle.astype(f32)).astype(bf16)


def six_products(left, right, product):
    rows = left[0].shape[0]
    first = product(jnp.concatenate(left, axis=0), right[0])
    second = product(jnp.concatenate(left[:2], axis=0), right[1])
    third = product(left[0], right[2])
    small = third + second[rows:] + first[2 * rows :]
    return first[:rows] + ((first[rows : 2 * rows] + second[:rows]) + small)


def mm6(left, right):
    return jnp.dot(left, right, preferred_element_type=f32, precision=highest)


def length_scale(depth):
    return 0.5 * 2.0 ** (depth / 8.0)


def features_kernel(
    emb_in, freq_in, phase_in, direction_in, feat, part_first, part,
    emb, freq, phase, direction, proj, keep, high, low, sems,
):
    loads = [
        pltpu.make_async_copy(source, target, sems.at[n])
        for n, (source, target) in enumerate(
            ((emb_in, emb), (freq_in, freq), (phase_in, phase), (direction_in, direction))
        )
    ]
    for load in loads:
        load.start()
    for load in loads:
        load.wait()
    proj[...] = mm(emb[...], freq[...])

    def chunk(step, carry):
        rows = pl.ds(pl.multiple_of(step * CHUNK, CHUNK), CHUNK)
        block = proj[rows, :]
        for level in range(LEVELS):
            angle = block * (1.0 / length_scale(level + 1)) + phase[level : level + 1, :]
            value = scaled_cosine(angle)
            keep[level, rows, :] = value
            high_part, low_part = split(value)
            high[level, rows, :] = high_part
            low[level, rows, :] = low_part
        pltpu.make_async_copy(keep.at[:, rows, :], feat.at[:, rows, :], sems.at[4]).start()
        return carry

    lax.fori_loop(0, LEAF // CHUNK, chunk, 0)
    direction_high, direction_low = split(direction[...])
    stacked = jnp.concatenate([direction_high, direction_low], axis=0)
    for level in range(LEVELS):
        both = mm(stacked, high[level])
        total = both[:ROWS] + (both[ROWS:] + mm(direction_high, low[level]))
        if level == 0:
            part_first[...] = total
        else:
            slot = 2 * (level - 1)
            part[pl.ds(slot, ROWS, stride=16), :] = total[:, :128]
            part[pl.ds(slot + 1, ROWS, stride=16), :] = total[:, 128:]
    pltpu.make_async_copy(keep, feat, sems.at[4]).wait()


def eye_block():
    row = lax.broadcasted_iota(jnp.int32, (HALF, HALF), 0)
    column = lax.broadcasted_iota(jnp.int32, (HALF, HALF), 1)
    return jnp.where(row == column, 1.0, 0.0).astype(f32)


def inverse_block(block, largest):
    eye = eye_block()
    start = 2.0 / (RIDGE + largest)
    scale = jnp.minimum((largest + RIDGE) / jnp.maximum(largest - RIDGE, 1e-3), 1e4)
    error = eye - start * block
    inverse = None
    for step in range(6):
        double = 2.0 * scale * scale
        gain = double / (double - 1.0)
        error_parts = split(error)
        if step == 0:
            inverse = (gain * start) * (eye + error)
        else:
            inverse = gain * (inverse + mm3(split(inverse), error_parts))
        if step < 5:
            error = gain * mm3(error_parts, error_parts) - (gain / double) * eye
            scale = jnp.minimum(double - 1.0, 1e4)
    block_parts = split(block)
    for step in range(3):
        if step < 2:
            error = eye - mm3(block_parts, split(inverse))
        else:
            error = eye - mm6(block, inverse)
        inverse_high, inverse_low = split(inverse)
        if step < 1:
            inverse = inverse + mm3((inverse_high, inverse_low), split(error))
        else:
            inverse = inverse + mm(inverse_high, error.astype(bf16))
    return inverse


def leaf_first_kernel(
    emb_in, direction_in, after, near, first_out, across_out, schur_out, largest_out,
    emb, direction, grid, matrix, sems,
):
    loads = [
        pltpu.make_async_copy(emb_in, emb, sems.at[0]),
        pltpu.make_async_copy(direction_in, direction, sems.at[1]),
    ]
    for load in loads:
        load.start()
    for load in loads:
        load.wait()
    points = emb[...]
    wide = points.astype(f32)
    square_high, square_low = split(wide * wide)
    ones_left = jnp.ones((8, EMBED), bf16)
    ones_right = jnp.ones((EMBED, 128), bf16)
    along = (mm_t(ones_left, square_high) + mm_t(ones_left, square_low))[:1, :]
    down = (mm(square_high, ones_right) + mm(square_low, ones_right))[:, :1]
    grid[...] = down + along
    matrix[...] = mm_t(points, points)

    def chunk(step, carry):
        begin = pl.multiple_of(step * CHUNK, CHUNK)
        rows = pl.ds(begin, CHUNK)
        distances = grid[rows, :] - 2.0 * matrix[rows, :]
        value = math.sqrt(RANK / LEAF) * jnp.exp(distances * (-1.0 / 0.5))
        row = begin + lax.broadcasted_iota(jnp.int32, (CHUNK, LEAF), 0)
        column = lax.broadcasted_iota(jnp.int32, (CHUNK, LEAF), 1)
        matrix[rows, :] = value + jnp.where(row == column, RIDGE, 0.0)
        return carry

    lax.fori_loop(0, LEAF // CHUNK, chunk, 0)
    near[...] = mm6(direction[...], matrix[...])
    sums = jnp.sum(matrix[...], axis=0, keepdims=True)
    largest = jnp.max(sums, axis=1, keepdims=True)
    largest_out[...] = jnp.broadcast_to(largest, (8, 128))
    side = matrix[:HALF, HALF:]
    first = inverse_block(matrix[:HALF, :HALF], largest)
    across = mm6(first, side)
    first_out[...] = first
    across_out[...] = across
    schur_out[...] = matrix[HALF:, HALF:] - mm6(jnp.transpose(across), side)


def leaf_second_kernel(first, across_in, schur, largest, residual_in, after, solved, inv, residual, sem):
    load = pltpu.make_async_copy(residual_in, residual, sem.at[0])
    load.start()
    across = across_in[...]
    second = inverse_block(schur[...], largest[:1, :1])
    lower = -mm6(second, jnp.transpose(across))
    top = first[...] - mm6(across, lower)
    left = jnp.concatenate([top, lower], axis=0)
    right = jnp.concatenate([jnp.transpose(lower), second], axis=0)
    for n, plane in enumerate(planes(left)):
        inv[n, :, :HALF] = plane
    for n, plane in enumerate(planes(right)):
        inv[n, :, HALF:] = plane
    load.wait()
    solved[...] = six_products(planes(residual[...]), [inv[n] for n in range(3)], mm)


def middle_send_kernel(received, out):
    total = received[0, 8:16, :]
    for source in range(1, PTS):
        total = total + received[source, 8:16, :]
    for target in range(GRP):
        out[target] = total


def row_select(tiles):
    row = lax.broadcasted_iota(jnp.int32, (8, 128), 0)
    return jnp.where(row < 2, tiles[0], jnp.where(row < 4, tiles[1], jnp.where(row < 6, tiles[2], tiles[3])))


def middle_return_kernel(place, received, wide, after, out):
    sums = [received[source, 0:8, :] for source in range(PTS)]
    stages = []
    for _ in range(5):
        sums = [sums[2 * n] + sums[2 * n + 1] for n in range(len(sums) // 2)]
        stages.append(sums)
    line = place[0]
    upper = []
    for depth in range(4):
        base = (line >> depth) << (depth + 1)
        total = wide[base] + wide[base + 1]
        for source in range(2, 2 ** (depth + 1)):
            total = total + wide[base + source]
        upper.append(total)
    top = row_select(upper)
    for node in range(8):
        low = row_select([stages[1][node], stages[2][node // 2], stages[3][node // 4], stages[4][0]])
        for leaf in range(4):
            out[node * 4 + leaf, 0:8, :] = low
            out[node * 4 + leaf, 8:16, :] = top


def image_kernel(
    own_first, other_first, returned, feat_in, near, direction_in, residual_in, solved, inv, image, shifted, out,
    feat, direction, residual, sems,
):
    loads = [pltpu.make_async_copy(feat_in.at[n], feat.at[n], sems.at[n]) for n in range(LEVELS)]
    loads.append(pltpu.make_async_copy(direction_in, direction, sems.at[LEVELS]))
    loads.append(pltpu.make_async_copy(residual_in, residual, sems.at[LEVELS + 1]))
    for load in loads:
        load.start()
    spread = near[...]
    for level in range(LEVELS):
        if level == 0:
            total = own_first[...] + other_first[...]
        else:
            slot = 2 * (level - 1)
            total = jnp.concatenate(
                [returned[pl.ds(slot, ROWS, stride=16), :], returned[pl.ds(slot + 1, ROWS, stride=16), :]],
                axis=1,
            )
        weight = math.sqrt(RANK / (LEAF * 2 ** (level + 1)))
        loads[level].wait()
        spread = spread + six_products(planes(total * weight), planes(feat[level]), mm_t)
    image[...] = spread
    moved = six_products(planes(spread), [inv[n] for n in range(3)], mm)
    shifted[...] = moved
    loads[LEVELS].wait()
    loads[LEVELS + 1].wait()
    first = solved[...]
    products = jnp.concatenate(
        [residual[...] * first, direction[...] * spread, first * spread, spread * moved], axis=0
    )
    folded = products[:, :128] + products[:, 128:256] + (products[:, 256:384] + products[:, 384:])
    out[...] = jnp.sum(jnp.transpose(folded), axis=0, keepdims=True)


def sum_spread_kernel(received, out):
    total = received[0]
    for source in range(1, PTS):
        total = total + received[source]
    for target in range(GRP):
        out[target] = total


def finish_kernel(received, solution, residual, direction, solved, image, shifted, new_solution, new_residual, new_direction):
    total = received[0]
    for source in range(1, GRP):
        total = total + received[source]
    row = lax.broadcasted_iota(jnp.int32, (ROWS, 128), 0)
    column = lax.broadcasted_iota(jnp.int32, (ROWS, 128), 1)
    spread = jnp.broadcast_to(total, (ROWS, 128))

    def pick(slot):
        return jnp.sum(jnp.where(column == row + ROWS * slot, spread, 0.0), axis=1, keepdims=True)

    norm_old, curvature, cross, moved = pick(0), pick(1), pick(2), pick(3)
    step = norm_old / curvature
    norm_new = norm_old - step * (2.0 * cross - step * moved)
    ratio = norm_new / norm_old
    direction_value = direction[...]
    new_solution[...] = solution[...] + step * direction_value
    new_residual[...] = residual[...] - step * image[...]
    new_direction[...] = (solved[...] - step * shifted[...]) + ratio * direction_value


def whole(shape, dtype=f32):
    return jax.ShapeDtypeStruct(shape, dtype)


def call(kernel, outs, *args, scratch=(), name=None, hbm=(), scalars=0, hbm_out=()):
    vmem = pl.BlockSpec(memory_space=pltpu.VMEM)
    smem = pl.BlockSpec(memory_space=pltpu.SMEM)
    far = pl.BlockSpec(memory_space=pltpu.HBM)
    anywhere = pl.BlockSpec(memory_space=pl.ANY)
    single = not isinstance(outs, (tuple, list))
    kinds = {"hbm": far, "any": anywhere}
    specs = [smem if n < scalars else vmem for n in range(len(args))]
    args = list(args)
    for place, kind in hbm:
        specs[place] = kinds[kind]
        if kind == "hbm":
            args[place] = pltpu.with_memory_space_constraint(args[place], pltpu.HBM)
    return pl.pallas_call(
        kernel,
        out_shape=outs,
        in_specs=specs,
        out_specs=vmem if single else tuple(far if n in hbm_out else vmem for n in range(len(outs))),
        scratch_shapes=list(scratch),
        compiler_params=pltpu.CompilerParams(vmem_limit_bytes=50 * 2**20),
        name=name,
    )(*args)


def exchange(value, axes):
    return lax.all_to_all(value, axes, 0, 0, tiled=True)


def body(embeddings, frequencies, phases, solution, residual, direction):
    rows = whole((ROWS, LEAF))
    half = whole((HALF, HALF))
    leaf_points = pltpu.VMEM((LEAF, EMBED), bf16)
    leaf_rows = pltpu.VMEM((ROWS, LEAF), f32)
    panel = pltpu.VMEM((LEVELS, LEAF, RANK), f32)
    feat, part_first, part = call(
        features_kernel,
        (whole((LEVELS, LEAF, RANK)), whole((ROWS, RANK)), whole((ROWS * 16, 128))),
        embeddings, frequencies, phases, direction,
        hbm=[(n, "hbm") for n in range(4)],
        hbm_out=(0,),
        scratch=(
            leaf_points,
            pltpu.VMEM((EMBED, RANK), bf16),
            pltpu.VMEM((LEVELS, RANK), f32),
            leaf_rows,
            pltpu.VMEM((LEAF, RANK), f32),
            panel,
            pltpu.VMEM((LEVELS, LEAF, RANK), bf16),
            pltpu.VMEM((LEVELS, LEAF, RANK), bf16),
            pltpu.SemaphoreType.DMA((5,)),
        ),
        name="features",
    )
    other_first = lax.ppermute(part_first, "z", [(n, n ^ 1) for n in range(8)])
    received = exchange(part.reshape(ROWS, 16, 128), ("x", "z"))
    middle = call(middle_send_kernel, whole((GRP, 8, 128)), received, name="middle_send")
    wide = exchange(middle, ("y", "c"))
    near, first, across, schur, largest = call(
        leaf_first_kernel, (rows, half, half, half, whole((8, 128))), embeddings, direction, middle,
        hbm=[(0, "hbm"), (1, "hbm"), (2, "any")],
        scratch=(
            leaf_points, leaf_rows, pltpu.VMEM((LEAF, LEAF), f32), pltpu.VMEM((LEAF, LEAF), f32),
            pltpu.SemaphoreType.DMA((2,)),
        ),
        name="leaf_first",
    )
    place = lax.axis_index("y").astype(jnp.int32).reshape(1)
    back = call(
        middle_return_kernel, whole((PTS, 16, 128)), place, received, wide, largest,
        hbm=[(3, "any")], scalars=1, name="middle_return",
    )
    returned = exchange(back, ("x", "z"))
    solved, inv = call(
        leaf_second_kernel, (rows, whole((3, LEAF, LEAF), bf16)), first, across, schur, largest, residual, back,
        hbm=[(4, "hbm"), (5, "any")], scratch=(leaf_rows, pltpu.SemaphoreType.DMA((1,))), name="leaf_second",
    )
    image, shifted, sums = call(
        image_kernel, (rows, rows, whole((1, 128))),
        part_first, other_first, returned.reshape(PTS * 16, 128), feat, near, direction, residual, solved, inv,
        hbm=[(3, "hbm"), (5, "hbm"), (6, "hbm")],
        scratch=(panel, leaf_rows, leaf_rows, pltpu.SemaphoreType.DMA((LEVELS + 2,))),
        name="image",
    )
    gathered = exchange(jnp.broadcast_to(sums[None], (PTS, 1, 128)), ("x", "z"))
    middle_sums = call(sum_spread_kernel, whole((GRP, 1, 128)), gathered, name="sum_spread")
    totals = exchange(middle_sums, ("y", "c"))
    return call(
        finish_kernel, (rows, rows, rows), totals, solution, residual, direction, solved, image, shifted, name="finish"
    )


def solution(mesh):
    torus = Mesh(mesh.devices.reshape(8, 2, 4, 8), AXES)
    columns = P(None, AXES)
    return jax.shard_map(
        body,
        mesh=torus,
        in_specs=(P(AXES, None), P(), P(), columns, columns, columns),
        out_specs=(columns, columns, columns),
        check_vma=False,
    )
```

```python
import math

import jax
import jax.numpy as jnp
import numpy as np
from jax import lax
from jax.experimental import pallas as pl
from jax.experimental.pallas import tpu as pltpu
from jax.sharding import Mesh
from jax.sharding import PartitionSpec as P

AXES = ("y", "c", "x", "z")
LEAF, EMBED, RANK, ROWS, LEVELS = 512, 768, 256, 32, 9
PTS, GRP = 32, 16
RIDGE = 0.5
HALF = LEAF // 2
CHUNK = 32

f32 = jnp.float32
bf16 = jnp.bfloat16
highest = lax.Precision.HIGHEST


COSINE_DEGREE = 6


def cosine_coefficients():
    cheb = np.polynomial.chebyshev
    nodes = np.cos(np.pi * (np.arange(64) + 0.5) / 64)
    series = cheb.chebfit(nodes, np.cos(2.0 * np.pi * np.sqrt((nodes + 1.0) / 8.0)), COSINE_DEGREE)
    poly = np.polynomial.Polynomial(cheb.cheb2poly(series))
    shifted = poly(np.polynomial.Polynomial([-1.0, 8.0]))
    return [float(value) for value in shifted.coef * math.sqrt(2.0 / RANK)]


COSINE = cosine_coefficients()
TURN = 2.0 * math.pi


def scaled_cosine(turns):
    part = turns - jnp.round(turns)
    square = part * part
    value = COSINE[-1] * square + COSINE[-2]
    for coefficient in COSINE[-3::-1]:
        value = value * square + coefficient
    return value


def split(value):
    high = value.astype(bf16)
    return high, (value - high.astype(f32)).astype(bf16)


def mm(left, right):
    return jnp.dot(left, right, preferred_element_type=f32)


def mm_t(left, right, precision=None):
    return lax.dot_general(
        left, right, (((1,), (1,)), ((), ())), preferred_element_type=f32, precision=precision
    )


def mm3(left, right):
    return mm(left[0], right[0]) + (mm(left[0], right[1]) + mm(left[1], right[0]))


def planes(value):
    high = value.astype(bf16)
    rest = value - high.astype(f32)
    middle = rest.astype(bf16)
    return high, middle, (rest - middle.astype(f32)).astype(bf16)


def six_products(left, right, product):
    rows = left[0].shape[0]
    first = product(jnp.concatenate(left, axis=0), right[0])
    second = product(jnp.concatenate(left[:2], axis=0), right[1])
    third = product(left[0], right[2])
    small = third + second[rows:] + first[2 * rows :]
    return first[:rows] + ((first[rows : 2 * rows] + second[:rows]) + small)


def mm6(left, right):
    return jnp.dot(left, right, preferred_element_type=f32, precision=highest)


def length_scale(depth):
    return 0.5 * 2.0 ** (depth / 8.0)


def features_kernel(
    emb_in, freq_in, phase_in, direction_in, feat, part_first, part,
    emb, freq, phase, direction, proj, keep, high, low, sems,
):
    loads = [
        pltpu.make_async_copy(source, target, sems.at[n])
        for n, (source, target) in enumerate(
            ((emb_in, emb), (freq_in, freq), (phase_in, phase), (direction_in, direction))
        )
    ]
    for load in loads:
        load.start()
    for load in loads:
        load.wait()
    proj[...] = mm(emb[...], freq[...])
    phase_turns = phase[...] * (1.0 / TURN)

    def chunk(step, carry):
        rows = pl.ds(pl.multiple_of(step * CHUNK, CHUNK), CHUNK)
        block = proj[rows, :]
        for level in range(LEVELS):
            turns = block * (1.0 / (TURN * length_scale(level + 1))) + phase_turns[level : level + 1, :]
            value = scaled_cosine(turns)
            keep[level, rows, :] = value
            high_part, low_part = split(value)
            high[level, rows, :] = high_part
            low[level, rows, :] = low_part
        pltpu.make_async_copy(keep.at[:, rows, :], feat.at[:, rows, :], sems.at[4]).start()
        return carry

    lax.fori_loop(0, LEAF // CHUNK, chunk, 0)
    direction_high, direction_low = split(direction[...])
    stacked = jnp.concatenate([direction_high, direction_low], axis=0)
    for level in range(LEVELS):
        both = mm(stacked, high[level])
        total = both[:ROWS] + (both[ROWS:] + mm(direction_high, low[level]))
        if level == 0:
            part_first[...] = total
        else:
            slot = 2 * (level - 1)
            part[pl.ds(slot, ROWS, stride=16), :] = total[:, :128]
            part[pl.ds(slot + 1, ROWS, stride=16), :] = total[:, 128:]
    pltpu.make_async_copy(keep, feat, sems.at[4]).wait()


def eye_block():
    row = lax.broadcasted_iota(jnp.int32, (HALF, HALF), 0)
    column = lax.broadcasted_iota(jnp.int32, (HALF, HALF), 1)
    return jnp.where(row == column, 1.0, 0.0).astype(f32)


def inverse_block(block, largest):
    eye = eye_block()
    start = 2.0 / (RIDGE + largest)
    scale = jnp.minimum((largest + RIDGE) / jnp.maximum(largest - RIDGE, 1e-3), 1e4)
    error = eye - start * block
    inverse = None
    for step in range(6):
        double = 2.0 * scale * scale
        gain = double / (double - 1.0)
        error_parts = split(error)
        if step == 0:
            inverse = (gain * start) * (eye + error)
        else:
            inverse = gain * (inverse + mm3(split(inverse), error_parts))
        if step < 5:
            error = gain * mm3(error_parts, error_parts) - (gain / double) * eye
            scale = jnp.minimum(double - 1.0, 1e4)
    block_parts = split(block)
    for step in range(2):
        if step < 1:
            error = eye - mm3(block_parts, split(inverse))
        else:
            error = eye - mm6(block, inverse)
        inverse = inverse + mm3(split(inverse), split(error))
    return inverse


def leaf_matrix_kernel(
    emb_in, direction_in, after, near, matrix, largest_out, emb, direction, grid, sems
):
    loads = [
        pltpu.make_async_copy(emb_in, emb, sems.at[0]),
        pltpu.make_async_copy(direction_in, direction, sems.at[1]),
    ]
    for load in loads:
        load.start()
    for load in loads:
        load.wait()
    points = emb[...]
    wide = points.astype(f32)
    square_high, square_low = split(wide * wide)
    ones_left = jnp.ones((8, EMBED), bf16)
    ones_right = jnp.ones((EMBED, 128), bf16)
    along = (mm_t(ones_left, square_high) + mm_t(ones_left, square_low))[:1, :]
    down = (mm(square_high, ones_right) + mm(square_low, ones_right))[:, :1]
    grid[...] = down + along
    matrix[...] = mm_t(points, points)

    def chunk(step, carry):
        begin = pl.multiple_of(step * CHUNK, CHUNK)
        rows = pl.ds(begin, CHUNK)
        distances = grid[rows, :] - 2.0 * matrix[rows, :]
        value = math.sqrt(RANK / LEAF) * jnp.exp(distances * (-1.0 / 0.5))
        row = begin + lax.broadcasted_iota(jnp.int32, (CHUNK, LEAF), 0)
        column = lax.broadcasted_iota(jnp.int32, (CHUNK, LEAF), 1)
        matrix[rows, :] = value + jnp.where(row == column, RIDGE, 0.0)
        return carry

    lax.fori_loop(0, LEAF // CHUNK, chunk, 0)
    near[...] = mm6(direction[...], matrix[...])
    sums = jnp.sum(matrix[...], axis=0, keepdims=True)
    largest = jnp.max(sums, axis=1, keepdims=True)
    largest_out[...] = jnp.broadcast_to(largest, (8, 128))


def leaf_first_kernel(matrix, largest, after, first_out, across_out, schur_out):
    side = matrix[:HALF, HALF:]
    first = inverse_block(matrix[:HALF, :HALF], largest[:1, :1])
    across = mm6(first, side)
    first_out[...] = first
    across_out[...] = across
    schur_out[...] = matrix[HALF:, HALF:] - mm6(jnp.transpose(across), side)


def leaf_second_kernel(
    first, across_in, schur, largest, matrix, residual_in, after, solved, inv, residual, whole_inverse, sem
):
    load = pltpu.make_async_copy(residual_in, residual, sem.at[0])
    load.start()
    across = across_in[...]
    second = inverse_block(schur[...], largest[:1, :1])
    lower = -mm6(second, jnp.transpose(across))
    top = first[...] - mm6(across, lower)
    whole_inverse[:HALF, :HALF] = top
    whole_inverse[HALF:, :HALF] = lower
    whole_inverse[:HALF, HALF:] = jnp.transpose(lower)
    whole_inverse[HALF:, HALF:] = second
    row = lax.broadcasted_iota(jnp.int32, (LEAF, LEAF), 0)
    column = lax.broadcasted_iota(jnp.int32, (LEAF, LEAF), 1)
    start = whole_inverse[...]
    start_planes = planes(start)
    error = jnp.where(row == column, 1.0, 0.0) - six_products(planes(matrix[...]), start_planes, mm)
    better = start + mm3(start_planes[:2], split(error))
    for n, plane in enumerate(planes(better)):
        inv[n] = plane
    load.wait()
    solved[...] = six_products(planes(residual[...]), [inv[n] for n in range(3)], mm)


def middle_send_kernel(received, first_after, second_after, out):
    total = received[0, 8:16, :]
    for source in range(1, PTS):
        total = total + received[source, 8:16, :]
    for target in range(GRP):
        out[target] = total


def row_select(tiles):
    row = lax.broadcasted_iota(jnp.int32, (8, 128), 0)
    return jnp.where(row < 2, tiles[0], jnp.where(row < 4, tiles[1], jnp.where(row < 6, tiles[2], tiles[3])))


def middle_return_kernel(place, received, wide, after, out):
    sums = [received[source, 0:8, :] for source in range(PTS)]
    stages = []
    for _ in range(5):
        sums = [sums[2 * n] + sums[2 * n + 1] for n in range(len(sums) // 2)]
        stages.append(sums)
    line = place[0]
    upper = []
    for depth in range(4):
        base = (line >> depth) << (depth + 1)
        total = wide[base] + wide[base + 1]
        for source in range(2, 2 ** (depth + 1)):
            total = total + wide[base + source]
        upper.append(total)
    top = row_select(upper)
    for node in range(8):
        low = row_select([stages[1][node], stages[2][node // 2], stages[3][node // 4], stages[4][0]])
        for leaf in range(4):
            out[node * 4 + leaf, 0:8, :] = low
            out[node * 4 + leaf, 8:16, :] = top


def image_kernel(
    own_first, other_first, returned, feat_in, near, direction_in, residual_in, solved, inv, image, shifted, out,
    feat, direction, residual, sems,
):
    loads = [pltpu.make_async_copy(feat_in.at[n], feat.at[n], sems.at[n]) for n in range(LEVELS)]
    loads.append(pltpu.make_async_copy(direction_in, direction, sems.at[LEVELS]))
    loads.append(pltpu.make_async_copy(residual_in, residual, sems.at[LEVELS + 1]))
    for load in loads:
        load.start()
    spread = near[...]
    for level in range(LEVELS):
        if level == 0:
            total = own_first[...] + other_first[...]
        else:
            slot = 2 * (level - 1)
            total = jnp.concatenate(
                [returned[pl.ds(slot, ROWS, stride=16), :], returned[pl.ds(slot + 1, ROWS, stride=16), :]],
                axis=1,
            )
        weight = math.sqrt(RANK / (LEAF * 2 ** (level + 1)))
        loads[level].wait()
        spread = spread + six_products(planes(total * weight), planes(feat[level]), mm_t)
    image[...] = spread
    moved = six_products(planes(spread), [inv[n] for n in range(3)], mm)
    shifted[...] = moved
    loads[LEVELS].wait()
    loads[LEVELS + 1].wait()
    first = solved[...]
    products = jnp.concatenate(
        [residual[...] * first, direction[...] * spread, first * spread, spread * moved], axis=0
    )
    folded = products[:, :128] + products[:, 128:256] + (products[:, 256:384] + products[:, 384:])
    out[...] = jnp.sum(jnp.transpose(folded), axis=0, keepdims=True)


def sum_spread_kernel(received, out):
    total = received[0]
    for source in range(1, PTS):
        total = total + received[source]
    for target in range(GRP):
        out[target] = total


def finish_kernel(received, solution, residual, direction, solved, image, shifted, new_solution, new_residual, new_direction):
    total = received[0]
    for source in range(1, GRP):
        total = total + received[source]
    row = lax.broadcasted_iota(jnp.int32, (ROWS, 128), 0)
    column = lax.broadcasted_iota(jnp.int32, (ROWS, 128), 1)
    spread = jnp.broadcast_to(total, (ROWS, 128))

    def pick(slot):
        return jnp.sum(jnp.where(column == row + ROWS * slot, spread, 0.0), axis=1, keepdims=True)

    norm_old, curvature, cross, moved = pick(0), pick(1), pick(2), pick(3)
    step = norm_old / curvature
    norm_new = norm_old - step * (2.0 * cross - step * moved)
    ratio = norm_new / norm_old
    direction_value = direction[...]
    new_solution[...] = solution[...] + step * direction_value
    new_residual[...] = residual[...] - step * image[...]
    new_direction[...] = (solved[...] - step * shifted[...]) + ratio * direction_value


def whole(shape, dtype=f32):
    return jax.ShapeDtypeStruct(shape, dtype)


def call(kernel, outs, *args, scratch=(), name=None, hbm=(), scalars=0, hbm_out=()):
    vmem = pl.BlockSpec(memory_space=pltpu.VMEM)
    smem = pl.BlockSpec(memory_space=pltpu.SMEM)
    far = pl.BlockSpec(memory_space=pltpu.HBM)
    anywhere = pl.BlockSpec(memory_space=pl.ANY)
    single = not isinstance(outs, (tuple, list))
    kinds = {"hbm": far, "any": anywhere}
    specs = [smem if n < scalars else vmem for n in range(len(args))]
    args = list(args)
    for place, kind in hbm:
        specs[place] = kinds[kind]
        if kind == "hbm":
            args[place] = pltpu.with_memory_space_constraint(args[place], pltpu.HBM)
    return pl.pallas_call(
        kernel,
        out_shape=outs,
        in_specs=specs,
        out_specs=vmem if single else tuple(far if n in hbm_out else vmem for n in range(len(outs))),
        scratch_shapes=list(scratch),
        compiler_params=pltpu.CompilerParams(vmem_limit_bytes=50 * 2**20),
        name=name,
    )(*args)


def exchange(value, axes):
    return lax.all_to_all(value, axes, 0, 0, tiled=True)


def body(embeddings, frequencies, phases, solution, residual, direction):
    rows = whole((ROWS, LEAF))
    half = whole((HALF, HALF))
    leaf_points = pltpu.VMEM((LEAF, EMBED), bf16)
    leaf_rows = pltpu.VMEM((ROWS, LEAF), f32)
    panel = pltpu.VMEM((LEVELS, LEAF, RANK), f32)
    feat, part_first, part = call(
        features_kernel,
        (whole((LEVELS, LEAF, RANK)), whole((ROWS, RANK)), whole((ROWS * 16, 128))),
        embeddings, frequencies, phases, direction,
        hbm=[(n, "hbm") for n in range(4)],
        hbm_out=(0,),
        scratch=(
            leaf_points,
            pltpu.VMEM((EMBED, RANK), bf16),
            pltpu.VMEM((LEVELS, RANK), f32),
            leaf_rows,
            pltpu.VMEM((LEAF, RANK), f32),
            panel,
            pltpu.VMEM((LEVELS, LEAF, RANK), bf16),
            pltpu.VMEM((LEVELS, LEAF, RANK), bf16),
            pltpu.SemaphoreType.DMA((5,)),
        ),
        name="features",
    )
    other_first = lax.ppermute(part_first, "z", [(n, n ^ 1) for n in range(8)])
    received = exchange(part.reshape(ROWS, 16, 128), ("x", "z"))
    near, matrix, largest = call(
        leaf_matrix_kernel, (rows, whole((LEAF, LEAF)), whole((8, 128))), embeddings, direction, part_first,
        hbm=[(0, "hbm"), (1, "hbm"), (2, "any")],
        scratch=(leaf_points, leaf_rows, pltpu.VMEM((LEAF, LEAF), f32), pltpu.SemaphoreType.DMA((2,))),
        name="leaf_matrix",
    )
    middle = call(
        middle_send_kernel, whole((GRP, 8, 128)), received, largest, other_first,
        hbm=[(1, "any"), (2, "any")], name="middle_send",
    )
    wide = exchange(middle, ("y", "c"))
    first, across, schur = call(
        leaf_first_kernel, (half, half, half), matrix, largest, middle, hbm=[(2, "any")], name="leaf_first"
    )
    place = lax.axis_index("y").astype(jnp.int32).reshape(1)
    back = call(
        middle_return_kernel, whole((PTS, 16, 128)), place, received, wide, schur,
        hbm=[(3, "any")], scalars=1, name="middle_return",
    )
    returned = exchange(back, ("x", "z"))
    solved, inv = call(
        leaf_second_kernel, (rows, whole((3, LEAF, LEAF), bf16)), first, across, schur, largest, matrix, residual, back,
        hbm=[(5, "hbm"), (6, "any")],
        scratch=(leaf_rows, pltpu.VMEM((LEAF, LEAF), f32), pltpu.SemaphoreType.DMA((1,))), name="leaf_second",
    )
    image, shifted, sums = call(
        image_kernel, (rows, rows, whole((1, 128))),
        part_first, other_first, returned.reshape(PTS * 16, 128), feat, near, direction, residual, solved, inv,
        hbm=[(3, "hbm"), (5, "hbm"), (6, "hbm")],
        scratch=(panel, leaf_rows, leaf_rows, pltpu.SemaphoreType.DMA((LEVELS + 2,))),
        name="image",
    )
    gathered = exchange(jnp.broadcast_to(sums[None], (PTS, 1, 128)), ("x", "z"))
    middle_sums = call(sum_spread_kernel, whole((GRP, 1, 128)), gathered, name="sum_spread")
    totals = exchange(middle_sums, ("y", "c"))
    return call(
        finish_kernel, (rows, rows, rows), totals, solution, residual, direction, solved, image, shifted, name="finish"
    )


def solution(mesh):
    torus = Mesh(mesh.devices.reshape(8, 2, 4, 8), AXES)
    columns = P(None, AXES)
    return jax.shard_map(
        body,
        mesh=torus,
        in_specs=(P(AXES, None), P(), P(), columns, columns, columns),
        out_specs=(columns, columns, columns),
        check_vma=False,
    )
```

```python
import math

import jax
import jax.numpy as jnp
import numpy as np
from jax import lax
from jax.experimental import pallas as pl
from jax.experimental.pallas import tpu as pltpu
from jax.sharding import Mesh
from jax.sharding import PartitionSpec as P

AXES = ("y", "c", "x", "z")
LEAF, EMBED, RANK, ROWS, LEVELS = 512, 768, 256, 32, 9
PTS, GRP = 32, 16
RIDGE = 0.5
HALF = LEAF // 2
CHUNK = 32

f32 = jnp.float32
bf16 = jnp.bfloat16
highest = lax.Precision.HIGHEST


COSINE_DEGREE = 6


def cosine_coefficients():
    cheb = np.polynomial.chebyshev
    nodes = np.cos(np.pi * (np.arange(64) + 0.5) / 64)
    series = cheb.chebfit(nodes, np.cos(2.0 * np.pi * np.sqrt((nodes + 1.0) / 8.0)), COSINE_DEGREE)
    poly = np.polynomial.Polynomial(cheb.cheb2poly(series))
    shifted = poly(np.polynomial.Polynomial([-1.0, 8.0]))
    return [float(value) for value in shifted.coef * math.sqrt(2.0 / RANK)]


COSINE = cosine_coefficients()
TURN = 2.0 * math.pi


def scaled_cosine(turns):
    part = turns - jnp.round(turns)
    square = part * part
    value = COSINE[-1] * square + COSINE[-2]
    for coefficient in COSINE[-3::-1]:
        value = value * square + coefficient
    return value


def split(value):
    high = value.astype(bf16)
    return high, (value - high.astype(f32)).astype(bf16)


def mm(left, right):
    return jnp.dot(left, right, preferred_element_type=f32)


def mm_t(left, right, precision=None):
    return lax.dot_general(
        left, right, (((1,), (1,)), ((), ())), preferred_element_type=f32, precision=precision
    )


def mm3(left, right):
    return mm(left[0], right[0]) + (mm(left[0], right[1]) + mm(left[1], right[0]))


def planes(value):
    high = value.astype(bf16)
    rest = value - high.astype(f32)
    middle = rest.astype(bf16)
    return high, middle, (rest - middle.astype(f32)).astype(bf16)


def six_products(left, right, product):
    rows = left[0].shape[0]
    first = product(jnp.concatenate(left, axis=0), right[0])
    second = product(jnp.concatenate(left[:2], axis=0), right[1])
    third = product(left[0], right[2])
    small = third + second[rows:] + first[2 * rows :]
    return first[:rows] + ((first[rows : 2 * rows] + second[:rows]) + small)


def mm6(left, right):
    return jnp.dot(left, right, preferred_element_type=f32, precision=highest)


def length_scale(depth):
    return 0.5 * 2.0 ** (depth / 8.0)


def features_kernel(
    emb_in, freq_in, phase_in, direction_in, feat, part_first, part,
    emb, freq, phase, direction, proj, keep, high, low, sems,
):
    loads = [
        pltpu.make_async_copy(source, target, sems.at[n])
        for n, (source, target) in enumerate(
            ((emb_in, emb), (freq_in, freq), (phase_in, phase), (direction_in, direction))
        )
    ]
    for load in loads:
        load.start()
    for load in loads:
        load.wait()
    proj[...] = mm(emb[...], freq[...])
    phase_turns = phase[...] * (1.0 / TURN)

    def chunk(step, carry):
        rows = pl.ds(pl.multiple_of(step * CHUNK, CHUNK), CHUNK)
        block = proj[rows, :]
        for level in range(LEVELS):
            turns = block * (1.0 / (TURN * length_scale(level + 1))) + phase_turns[level : level + 1, :]
            value = scaled_cosine(turns)
            keep[level, rows, :] = value
            high_part, low_part = split(value)
            high[level, rows, :] = high_part
            low[level, rows, :] = low_part
        pltpu.make_async_copy(keep.at[:, rows, :], feat.at[:, rows, :], sems.at[4]).start()
        return carry

    lax.fori_loop(0, LEAF // CHUNK, chunk, 0)
    direction_high, direction_low = split(direction[...])
    stacked = jnp.concatenate([direction_high, direction_low], axis=0)
    for level in range(LEVELS):
        both = mm(stacked, high[level])
        total = both[:ROWS] + (both[ROWS:] + mm(direction_high, low[level]))
        if level == 0:
            part_first[...] = total
        else:
            slot = 2 * (level - 1)
            part[pl.ds(slot, ROWS, stride=16), :] = total[:, :128]
            part[pl.ds(slot + 1, ROWS, stride=16), :] = total[:, 128:]
    pltpu.make_async_copy(keep, feat, sems.at[4]).wait()


def eye_block():
    row = lax.broadcasted_iota(jnp.int32, (HALF, HALF), 0)
    column = lax.broadcasted_iota(jnp.int32, (HALF, HALF), 1)
    return jnp.where(row == column, 1.0, 0.0).astype(f32)


def inverse_block(block, largest):
    eye = eye_block()
    start = 2.0 / (RIDGE + largest)
    scale = jnp.minimum((largest + RIDGE) / jnp.maximum(largest - RIDGE, 1e-3), 1e4)
    error = eye - start * block
    inverse = None
    for step in range(7):
        double = 2.0 * scale * scale
        gain = double / (double - 1.0)
        error_parts = split(error)
        if step == 0:
            inverse = (gain * start) * (eye + error)
        else:
            inverse = gain * (inverse + mm3(split(inverse), error_parts))
        if step < 6:
            error = gain * mm3(error_parts, error_parts) - (gain / double) * eye
            scale = jnp.minimum(double - 1.0, 1e4)
    error = eye - mm6(block, inverse)
    inverse = inverse + mm3(split(inverse), split(error))
    return inverse


def leaf_matrix_kernel(
    emb_in, direction_in, after, near, matrix, largest_out, emb, direction, grid, sems
):
    loads = [
        pltpu.make_async_copy(emb_in, emb, sems.at[0]),
        pltpu.make_async_copy(direction_in, direction, sems.at[1]),
    ]
    for load in loads:
        load.start()
    for load in loads:
        load.wait()
    points = emb[...]
    wide = points.astype(f32)
    square_high, square_low = split(wide * wide)
    ones_left = jnp.ones((8, EMBED), bf16)
    ones_right = jnp.ones((EMBED, 128), bf16)
    along = (mm_t(ones_left, square_high) + mm_t(ones_left, square_low))[:1, :]
    down = (mm(square_high, ones_right) + mm(square_low, ones_right))[:, :1]
    grid[...] = down + along
    matrix[...] = mm_t(points, points)

    def chunk(step, carry):
        begin = pl.multiple_of(step * CHUNK, CHUNK)
        rows = pl.ds(begin, CHUNK)
        distances = grid[rows, :] - 2.0 * matrix[rows, :]
        value = math.sqrt(RANK / LEAF) * jnp.exp(distances * (-1.0 / 0.5))
        row = begin + lax.broadcasted_iota(jnp.int32, (CHUNK, LEAF), 0)
        column = lax.broadcasted_iota(jnp.int32, (CHUNK, LEAF), 1)
        matrix[rows, :] = value + jnp.where(row == column, RIDGE, 0.0)
        return carry

    lax.fori_loop(0, LEAF // CHUNK, chunk, 0)
    near[...] = mm6(direction[...], matrix[...])
    sums = jnp.sum(matrix[...], axis=0, keepdims=True)
    largest = jnp.max(sums, axis=1, keepdims=True)
    largest_out[...] = jnp.broadcast_to(largest, (8, 128))


def leaf_first_kernel(matrix, largest, after, first_out, across_out, schur_out, first_keep, across_keep, sems):
    side = matrix[:HALF, HALF:]
    first = inverse_block(matrix[:HALF, :HALF], largest[:1, :1])
    first_keep[...] = first
    across = mm6(first, side)
    across_keep[...] = across
    stores = [
        pltpu.make_async_copy(first_keep, first_out, sems.at[0]),
        pltpu.make_async_copy(across_keep, across_out, sems.at[1]),
    ]
    for store in stores:
        store.start()
    schur_out[...] = matrix[HALF:, HALF:] - mm6(jnp.transpose(across), side)
    for store in stores:
        store.wait()


def leaf_second_kernel(
    first_in, across_in, schur, largest, matrix, residual_in, after, solved, inv,
    first, across_scratch, residual, whole_inverse, sems,
):
    loads = [
        pltpu.make_async_copy(source, target, sems.at[n])
        for n, (source, target) in enumerate(
            ((first_in, first), (across_in, across_scratch), (residual_in, residual))
        )
    ]
    for load in loads:
        load.start()
    second = inverse_block(schur[...], largest[:1, :1])
    for load in loads:
        load.wait()
    across = across_scratch[...]
    lower = -mm6(second, jnp.transpose(across))
    top = first[...] - mm6(across, lower)
    whole_inverse[:HALF, :HALF] = top
    whole_inverse[HALF:, :HALF] = lower
    whole_inverse[:HALF, HALF:] = jnp.transpose(lower)
    whole_inverse[HALF:, HALF:] = second
    row = lax.broadcasted_iota(jnp.int32, (LEAF, LEAF), 0)
    column = lax.broadcasted_iota(jnp.int32, (LEAF, LEAF), 1)
    start = whole_inverse[...]
    start_planes = planes(start)
    error = jnp.where(row == column, 1.0, 0.0) - six_products(planes(matrix[...]), start_planes, mm)
    error_high = error.astype(bf16)
    better = start + (mm(start_planes[0], error_high) + mm(start_planes[1], error_high))
    for n, plane in enumerate(planes(better)):
        inv[n] = plane
    solved[...] = six_products(planes(residual[...]), [inv[n] for n in range(3)], mm)


def middle_send_kernel(received, first_after, second_after, out):
    total = received[0, 8:16, :]
    for source in range(1, PTS):
        total = total + received[source, 8:16, :]
    for target in range(GRP):
        out[target] = total


def row_select(tiles):
    row = lax.broadcasted_iota(jnp.int32, (8, 128), 0)
    return jnp.where(row < 2, tiles[0], jnp.where(row < 4, tiles[1], jnp.where(row < 6, tiles[2], tiles[3])))


def middle_return_kernel(place, received, wide, after, out):
    sums = [received[source, 0:8, :] for source in range(PTS)]
    stages = []
    for _ in range(5):
        sums = [sums[2 * n] + sums[2 * n + 1] for n in range(len(sums) // 2)]
        stages.append(sums)
    line = place[0]
    upper = []
    for depth in range(4):
        base = (line >> depth) << (depth + 1)
        total = wide[base] + wide[base + 1]
        for source in range(2, 2 ** (depth + 1)):
            total = total + wide[base + source]
        upper.append(total)
    top = row_select(upper)
    for node in range(8):
        low = row_select([stages[1][node], stages[2][node // 2], stages[3][node // 4], stages[4][0]])
        for leaf in range(4):
            out[node * 4 + leaf, 0:8, :] = low
            out[node * 4 + leaf, 8:16, :] = top


def image_kernel(
    own_first, other_first, returned, feat_in, near, direction_in, residual_in, solved, inv, image, shifted, out,
    feat, direction, residual, sems,
):
    loads = [pltpu.make_async_copy(feat_in.at[n], feat.at[n], sems.at[n]) for n in range(LEVELS)]
    loads.append(pltpu.make_async_copy(direction_in, direction, sems.at[LEVELS]))
    loads.append(pltpu.make_async_copy(residual_in, residual, sems.at[LEVELS + 1]))
    for load in loads:
        load.start()
    spread = near[...]
    for level in range(LEVELS):
        if level == 0:
            total = own_first[...] + other_first[...]
        else:
            slot = 2 * (level - 1)
            total = jnp.concatenate(
                [returned[pl.ds(slot, ROWS, stride=16), :], returned[pl.ds(slot + 1, ROWS, stride=16), :]],
                axis=1,
            )
        weight = math.sqrt(RANK / (LEAF * 2 ** (level + 1)))
        loads[level].wait()
        spread = spread + six_products(planes(total * weight), planes(feat[level]), mm_t)
    image[...] = spread
    moved = six_products(planes(spread), [inv[n] for n in range(3)], mm)
    shifted[...] = moved
    loads[LEVELS].wait()
    loads[LEVELS + 1].wait()
    first = solved[...]
    products = jnp.concatenate(
        [residual[...] * first, direction[...] * spread, first * spread, spread * moved], axis=0
    )
    folded = products[:, :128] + products[:, 128:256] + (products[:, 256:384] + products[:, 384:])
    out[...] = jnp.sum(jnp.transpose(folded), axis=0, keepdims=True)


def sum_spread_kernel(received, out):
    total = received[0]
    for source in range(1, PTS):
        total = total + received[source]
    for target in range(GRP):
        out[target] = total


def finish_kernel(received, solution, residual, direction, solved, image, shifted, new_solution, new_residual, new_direction):
    total = received[0]
    for source in range(1, GRP):
        total = total + received[source]
    row = lax.broadcasted_iota(jnp.int32, (ROWS, 128), 0)
    column = lax.broadcasted_iota(jnp.int32, (ROWS, 128), 1)
    spread = jnp.broadcast_to(total, (ROWS, 128))

    def pick(slot):
        return jnp.sum(jnp.where(column == row + ROWS * slot, spread, 0.0), axis=1, keepdims=True)

    norm_old, curvature, cross, moved = pick(0), pick(1), pick(2), pick(3)
    step = norm_old / curvature
    norm_new = norm_old - step * (2.0 * cross - step * moved)
    ratio = norm_new / norm_old
    direction_value = direction[...]
    new_solution[...] = solution[...] + step * direction_value
    new_residual[...] = residual[...] - step * image[...]
    new_direction[...] = (solved[...] - step * shifted[...]) + ratio * direction_value


def whole(shape, dtype=f32):
    return jax.ShapeDtypeStruct(shape, dtype)


def call(kernel, outs, *args, scratch=(), name=None, hbm=(), scalars=0, hbm_out=()):
    vmem = pl.BlockSpec(memory_space=pltpu.VMEM)
    smem = pl.BlockSpec(memory_space=pltpu.SMEM)
    far = pl.BlockSpec(memory_space=pltpu.HBM)
    anywhere = pl.BlockSpec(memory_space=pl.ANY)
    single = not isinstance(outs, (tuple, list))
    kinds = {"hbm": far, "any": anywhere}
    specs = [smem if n < scalars else vmem for n in range(len(args))]
    args = list(args)
    for place, kind in hbm:
        specs[place] = kinds[kind]
        if kind == "hbm":
            args[place] = pltpu.with_memory_space_constraint(args[place], pltpu.HBM)
    return pl.pallas_call(
        kernel,
        out_shape=outs if single else tuple(
            pltpu.HBM(out.shape, out.dtype) if n in hbm_out else out for n, out in enumerate(outs)
        ),
        in_specs=specs,
        out_specs=vmem if single else tuple(far if n in hbm_out else vmem for n in range(len(outs))),
        scratch_shapes=list(scratch),
        compiler_params=pltpu.CompilerParams(vmem_limit_bytes=50 * 2**20),
        name=name,
    )(*args)


def exchange(value, axes):
    return lax.all_to_all(value, axes, 0, 0, tiled=True)


def body(embeddings, frequencies, phases, solution, residual, direction):
    rows = whole((ROWS, LEAF))
    half = whole((HALF, HALF))
    leaf_points = pltpu.VMEM((LEAF, EMBED), bf16)
    leaf_rows = pltpu.VMEM((ROWS, LEAF), f32)
    block = pltpu.VMEM((HALF, HALF), f32)
    panel = pltpu.VMEM((LEVELS, LEAF, RANK), f32)
    feat, part_first, part = call(
        features_kernel,
        (whole((LEVELS, LEAF, RANK)), whole((ROWS, RANK)), whole((ROWS * 16, 128))),
        embeddings, frequencies, phases, direction,
        hbm=[(n, "hbm") for n in range(4)],
        hbm_out=(0,),
        scratch=(
            leaf_points,
            pltpu.VMEM((EMBED, RANK), bf16),
            pltpu.VMEM((LEVELS, RANK), f32),
            leaf_rows,
            pltpu.VMEM((LEAF, RANK), f32),
            panel,
            pltpu.VMEM((LEVELS, LEAF, RANK), bf16),
            pltpu.VMEM((LEVELS, LEAF, RANK), bf16),
            pltpu.SemaphoreType.DMA((5,)),
        ),
        name="features",
    )
    other_first = lax.ppermute(part_first, "z", [(n, n ^ 1) for n in range(8)])
    received = exchange(part.reshape(ROWS, 16, 128), ("x", "z"))
    near, matrix, largest = call(
        leaf_matrix_kernel, (rows, whole((LEAF, LEAF)), whole((8, 128))), embeddings, direction, part_first,
        hbm=[(0, "hbm"), (1, "hbm"), (2, "any")],
        scratch=(leaf_points, leaf_rows, pltpu.VMEM((LEAF, LEAF), f32), pltpu.SemaphoreType.DMA((2,))),
        name="leaf_matrix",
    )
    middle = call(
        middle_send_kernel, whole((GRP, 8, 128)), received, largest, other_first,
        hbm=[(1, "any"), (2, "any")], name="middle_send",
    )
    wide = exchange(middle, ("y", "c"))
    first, across, schur = call(
        leaf_first_kernel, (half, half, half), matrix, largest, middle, hbm=[(2, "any")], hbm_out=(0, 1),
        scratch=(block, block, pltpu.SemaphoreType.DMA((2,))), name="leaf_first",
    )
    place = lax.axis_index("y").astype(jnp.int32).reshape(1)
    back = call(
        middle_return_kernel, whole((PTS, 16, 128)), place, received, wide, schur,
        hbm=[(3, "any")], scalars=1, name="middle_return",
    )
    returned = exchange(back, ("x", "z"))
    solved, inv = call(
        leaf_second_kernel, (rows, whole((3, LEAF, LEAF), bf16)), first, across, schur, largest, matrix, residual, back,
        hbm=[(0, "hbm"), (1, "hbm"), (5, "hbm"), (6, "any")],
        scratch=(block, block, leaf_rows, pltpu.VMEM((LEAF, LEAF), f32), pltpu.SemaphoreType.DMA((3,))),
        name="leaf_second",
    )
    image, shifted, sums = call(
        image_kernel, (rows, rows, whole((1, 128))),
        part_first, other_first, returned.reshape(PTS * 16, 128), feat, near, direction, residual, solved, inv,
        hbm=[(3, "hbm"), (5, "hbm"), (6, "hbm")],
        scratch=(panel, leaf_rows, leaf_rows, pltpu.SemaphoreType.DMA((LEVELS + 2,))),
        name="image",
    )
    gathered = exchange(jnp.broadcast_to(sums[None], (PTS, 1, 128)), ("x", "z"))
    middle_sums = call(sum_spread_kernel, whole((GRP, 1, 128)), gathered, name="sum_spread")
    totals = exchange(middle_sums, ("y", "c"))
    return call(
        finish_kernel, (rows, rows, rows), totals, solution, residual, direction, solved, image, shifted, name="finish"
    )


def solution(mesh):
    torus = Mesh(mesh.devices.reshape(8, 2, 4, 8), AXES)
    columns = P(None, AXES)
    return jax.shard_map(
        body,
        mesh=torus,
        in_specs=(P(AXES, None), P(), P(), columns, columns, columns),
        out_specs=(columns, columns, columns),
        check_vma=False,
    )
```

```python
import math

import jax
import jax.numpy as jnp
import numpy as np
from jax import lax
from jax.experimental import pallas as pl
from jax.experimental.pallas import tpu as pltpu
from jax.sharding import Mesh
from jax.sharding import PartitionSpec as P

AXES = ("y", "c", "x", "z")
LEAF, EMBED, RANK, ROWS, LEVELS = 512, 768, 256, 32, 9
PTS, GRP = 32, 16
RIDGE = 0.5
HALF = LEAF // 2
CHUNK = 32

f32 = jnp.float32
bf16 = jnp.bfloat16
highest = lax.Precision.HIGHEST


SINE_DEGREE = 4
PEAK = math.sqrt(2.0 / RANK)


def sine_coefficients():
    cheb = np.polynomial.chebyshev
    nodes = np.cos(np.pi * (np.arange(64) + 0.5) / 64)
    part = np.sqrt((nodes + 1.0) / 8.0)
    series = cheb.chebfit(nodes, np.sin(np.pi * part) / part, SINE_DEGREE)
    poly = np.polynomial.Polynomial(cheb.cheb2poly(series))
    shifted = poly(np.polynomial.Polynomial([-1.0, 8.0]))
    return [float(value) for value in shifted.coef * math.sqrt(2.0 * PEAK)]


SINE = sine_coefficients()
TURN = 2.0 * math.pi


def scaled_cosine(turns):
    part = turns - jnp.round(turns)
    square = part * part
    value = SINE[-1] * square + SINE[-2]
    for coefficient in SINE[-3::-1]:
        value = value * square + coefficient
    sine = value * part
    return PEAK - sine * sine


def split(value):
    high = value.astype(bf16)
    return high, (value - high.astype(f32)).astype(bf16)


def mm(left, right):
    return jnp.dot(left, right, preferred_element_type=f32)


def mm_t(left, right, precision=None):
    return lax.dot_general(
        left, right, (((1,), (1,)), ((), ())), preferred_element_type=f32, precision=precision
    )


def mm3(left, right):
    return mm(left[0], right[0]) + (mm(left[0], right[1]) + mm(left[1], right[0]))


def planes(value):
    high = value.astype(bf16)
    rest = value - high.astype(f32)
    middle = rest.astype(bf16)
    return high, middle, (rest - middle.astype(f32)).astype(bf16)


def six_products(left, right, product):
    rows = left[0].shape[0]
    first = product(jnp.concatenate(left, axis=0), right[0])
    second = product(jnp.concatenate(left[:2], axis=0), right[1])
    third = product(left[0], right[2])
    small = third + second[rows:] + first[2 * rows :]
    return first[:rows] + ((first[rows : 2 * rows] + second[:rows]) + small)


def mm6(left, right):
    return jnp.dot(left, right, preferred_element_type=f32, precision=highest)


def length_scale(depth):
    return 0.5 * 2.0 ** (depth / 8.0)


def features_kernel(
    emb_in, freq_in, phase_in, direction_in, feat, part_first, part,
    emb, freq, phase, direction, proj, keep, high, low, sems,
):
    loads = [
        pltpu.make_async_copy(source, target, sems.at[n])
        for n, (source, target) in enumerate(
            ((emb_in, emb), (freq_in, freq), (phase_in, phase), (direction_in, direction))
        )
    ]
    for load in loads:
        load.start()
    for load in loads:
        load.wait()
    proj[...] = mm(emb[...], freq[...])
    phase_turns = phase[...] * (1.0 / TURN)

    def chunk(step, carry):
        rows = pl.ds(pl.multiple_of(step * CHUNK, CHUNK), CHUNK)
        block = proj[rows, :]
        for level in range(LEVELS):
            turns = block * (1.0 / (TURN * length_scale(level + 1))) + phase_turns[level : level + 1, :]
            value = scaled_cosine(turns)
            keep[level, rows, :] = value
            high_part, low_part = split(value)
            high[level, rows, :] = high_part
            low[level, rows, :] = low_part
        pltpu.make_async_copy(keep.at[:, rows, :], feat.at[:, rows, :], sems.at[4]).start()
        return carry

    lax.fori_loop(0, LEAF // CHUNK, chunk, 0)
    direction_high, direction_low = split(direction[...])
    stacked = jnp.concatenate([direction_high, direction_low], axis=0)
    for level in range(LEVELS):
        both = mm(stacked, high[level])
        total = both[:ROWS] + (both[ROWS:] + mm(direction_high, low[level]))
        if level == 0:
            part_first[...] = total
        else:
            slot = 2 * (level - 1)
            part[pl.ds(slot, ROWS, stride=16), :] = total[:, :128]
            part[pl.ds(slot + 1, ROWS, stride=16), :] = total[:, 128:]
    pltpu.make_async_copy(keep, feat, sems.at[4]).wait()


def eye_block():
    row = lax.broadcasted_iota(jnp.int32, (HALF, HALF), 0)
    column = lax.broadcasted_iota(jnp.int32, (HALF, HALF), 1)
    return jnp.where(row == column, 1.0, 0.0).astype(f32)


def inverse_block(block, largest):
    eye = eye_block()
    start = 2.0 / (RIDGE + largest)
    scale = jnp.minimum((largest + RIDGE) / jnp.maximum(largest - RIDGE, 1e-3), 1e4)
    error = eye - start * block
    inverse = None
    for step in range(7):
        double = 2.0 * scale * scale
        gain = double / (double - 1.0)
        error_parts = split(error)
        if step == 0:
            inverse = (gain * start) * (eye + error)
        else:
            inverse = gain * (inverse + mm3(split(inverse), error_parts))
        if step < 6:
            error = gain * mm3(error_parts, error_parts) - (gain / double) * eye
            scale = jnp.minimum(double - 1.0, 1e4)
    error = eye - mm6(block, inverse)
    inverse = inverse + mm3(split(inverse), split(error))
    return inverse


def leaf_matrix_kernel(
    emb_in, direction_in, after, near, matrix, largest_out, emb, direction, grid, sems
):
    loads = [
        pltpu.make_async_copy(emb_in, emb, sems.at[0]),
        pltpu.make_async_copy(direction_in, direction, sems.at[1]),
    ]
    for load in loads:
        load.start()
    for load in loads:
        load.wait()
    points = emb[...]
    wide = points.astype(f32)
    square_high, square_low = split(wide * wide)
    ones_left = jnp.ones((8, EMBED), bf16)
    ones_right = jnp.ones((EMBED, 128), bf16)
    along = (mm_t(ones_left, square_high) + mm_t(ones_left, square_low))[:1, :]
    down = (mm(square_high, ones_right) + mm(square_low, ones_right))[:, :1]
    grid[...] = down + along
    matrix[...] = mm_t(points, points)

    def chunk(step, carry):
        begin = pl.multiple_of(step * CHUNK, CHUNK)
        rows = pl.ds(begin, CHUNK)
        distances = grid[rows, :] - 2.0 * matrix[rows, :]
        value = math.sqrt(RANK / LEAF) * jnp.exp(distances * (-1.0 / 0.5))
        row = begin + lax.broadcasted_iota(jnp.int32, (CHUNK, LEAF), 0)
        column = lax.broadcasted_iota(jnp.int32, (CHUNK, LEAF), 1)
        matrix[rows, :] = value + jnp.where(row == column, RIDGE, 0.0)
        return carry

    lax.fori_loop(0, LEAF // CHUNK, chunk, 0)
    near[...] = mm6(direction[...], matrix[...])
    sums = jnp.sum(matrix[...], axis=0, keepdims=True)
    largest = jnp.max(sums, axis=1, keepdims=True)
    largest_out[...] = jnp.broadcast_to(largest, (8, 128))


def leaf_first_kernel(matrix, largest, after, first_out, across_out, schur_out, first_keep, across_keep, sems):
    side = matrix[:HALF, HALF:]
    first = inverse_block(matrix[:HALF, :HALF], largest[:1, :1])
    first_keep[...] = first
    across = mm6(first, side)
    across_keep[...] = across
    stores = [
        pltpu.make_async_copy(first_keep, first_out, sems.at[0]),
        pltpu.make_async_copy(across_keep, across_out, sems.at[1]),
    ]
    for store in stores:
        store.start()
    schur_out[...] = matrix[HALF:, HALF:] - mm6(jnp.transpose(across), side)
    for store in stores:
        store.wait()


def leaf_second_kernel(
    first_in, across_in, schur, largest, matrix, residual_in, after, solved, inv,
    first, across_scratch, residual, whole_inverse, sems,
):
    loads = [
        pltpu.make_async_copy(source, target, sems.at[n])
        for n, (source, target) in enumerate(
            ((first_in, first), (across_in, across_scratch), (residual_in, residual))
        )
    ]
    for load in loads:
        load.start()
    second = inverse_block(schur[...], largest[:1, :1])
    for load in loads:
        load.wait()
    across = across_scratch[...]
    lower = -mm6(second, jnp.transpose(across))
    top = first[...] - mm6(across, lower)
    whole_inverse[:HALF, :HALF] = top
    whole_inverse[HALF:, :HALF] = lower
    whole_inverse[:HALF, HALF:] = jnp.transpose(lower)
    whole_inverse[HALF:, HALF:] = second
    row = lax.broadcasted_iota(jnp.int32, (LEAF, LEAF), 0)
    column = lax.broadcasted_iota(jnp.int32, (LEAF, LEAF), 1)
    start = whole_inverse[...]
    start_planes = planes(start)
    error = jnp.where(row == column, 1.0, 0.0) - six_products(planes(matrix[...]), start_planes, mm)
    error_high = error.astype(bf16)
    better = start + (mm(start_planes[0], error_high) + mm(start_planes[1], error_high))
    for n, plane in enumerate(planes(better)):
        inv[n] = plane
    solved[...] = six_products(planes(residual[...]), [inv[n] for n in range(3)], mm)


def middle_send_kernel(received, first_after, second_after, out):
    total = received[0, 8:16, :]
    for source in range(1, PTS):
        total = total + received[source, 8:16, :]
    for target in range(GRP):
        out[target] = total


def row_select(tiles):
    row = lax.broadcasted_iota(jnp.int32, (8, 128), 0)
    return jnp.where(row < 2, tiles[0], jnp.where(row < 4, tiles[1], jnp.where(row < 6, tiles[2], tiles[3])))


def middle_return_kernel(place, received, wide, after, out):
    sums = [received[source, 0:8, :] for source in range(PTS)]
    stages = []
    for _ in range(5):
        sums = [sums[2 * n] + sums[2 * n + 1] for n in range(len(sums) // 2)]
        stages.append(sums)
    line = place[0]
    upper = []
    for depth in range(4):
        base = (line >> depth) << (depth + 1)
        total = wide[base] + wide[base + 1]
        for source in range(2, 2 ** (depth + 1)):
            total = total + wide[base + source]
        upper.append(total)
    top = row_select(upper)
    for node in range(8):
        low = row_select([stages[1][node], stages[2][node // 2], stages[3][node // 4], stages[4][0]])
        for leaf in range(4):
            out[node * 4 + leaf, 0:8, :] = low
            out[node * 4 + leaf, 8:16, :] = top


def image_kernel(
    own_first, other_first, returned, feat_in, near, direction_in, residual_in, solved, inv, image, shifted, out,
    feat, direction, residual, sems,
):
    loads = [pltpu.make_async_copy(feat_in.at[n], feat.at[n], sems.at[n]) for n in range(LEVELS)]
    loads.append(pltpu.make_async_copy(direction_in, direction, sems.at[LEVELS]))
    loads.append(pltpu.make_async_copy(residual_in, residual, sems.at[LEVELS + 1]))
    for load in loads:
        load.start()
    spread = near[...]
    for level in range(LEVELS):
        if level == 0:
            total = own_first[...] + other_first[...]
        else:
            slot = 2 * (level - 1)
            total = jnp.concatenate(
                [returned[pl.ds(slot, ROWS, stride=16), :], returned[pl.ds(slot + 1, ROWS, stride=16), :]],
                axis=1,
            )
        weight = math.sqrt(RANK / (LEAF * 2 ** (level + 1)))
        loads[level].wait()
        spread = spread + six_products(planes(total * weight), planes(feat[level]), mm_t)
    image[...] = spread
    moved = six_products(planes(spread), [inv[n] for n in range(3)], mm)
    shifted[...] = moved
    loads[LEVELS].wait()
    loads[LEVELS + 1].wait()
    first = solved[...]
    products = jnp.concatenate(
        [residual[...] * first, direction[...] * spread, first * spread, spread * moved], axis=0
    )
    folded = products[:, :128] + products[:, 128:256] + (products[:, 256:384] + products[:, 384:])
    out[...] = jnp.sum(jnp.transpose(folded), axis=0, keepdims=True)


def sum_spread_kernel(received, out):
    total = received[0]
    for source in range(1, GRP):
        total = total + received[source]
    for target in range(PTS):
        out[target] = total


def finish_kernel(received, solution, residual, direction, solved, image, shifted, new_solution, new_residual, new_direction):
    total = received[0]
    for source in range(1, PTS):
        total = total + received[source]
    row = lax.broadcasted_iota(jnp.int32, (ROWS, 128), 0)
    column = lax.broadcasted_iota(jnp.int32, (ROWS, 128), 1)
    spread = jnp.broadcast_to(total, (ROWS, 128))

    def pick(slot):
        return jnp.sum(jnp.where(column == row + ROWS * slot, spread, 0.0), axis=1, keepdims=True)

    norm_old, curvature, cross, moved = pick(0), pick(1), pick(2), pick(3)
    step = norm_old / curvature
    norm_new = norm_old - step * (2.0 * cross - step * moved)
    ratio = norm_new / norm_old
    direction_value = direction[...]
    new_solution[...] = solution[...] + step * direction_value
    new_residual[...] = residual[...] - step * image[...]
    new_direction[...] = (solved[...] - step * shifted[...]) + ratio * direction_value


def whole(shape, dtype=f32):
    return jax.ShapeDtypeStruct(shape, dtype)


def call(kernel, outs, *args, scratch=(), name=None, hbm=(), scalars=0, hbm_out=()):
    vmem = pl.BlockSpec(memory_space=pltpu.VMEM)
    smem = pl.BlockSpec(memory_space=pltpu.SMEM)
    far = pl.BlockSpec(memory_space=pltpu.HBM)
    anywhere = pl.BlockSpec(memory_space=pl.ANY)
    single = not isinstance(outs, (tuple, list))
    kinds = {"hbm": far, "any": anywhere}
    specs = [smem if n < scalars else vmem for n in range(len(args))]
    args = list(args)
    for place, kind in hbm:
        specs[place] = kinds[kind]
        if kind == "hbm":
            args[place] = pltpu.with_memory_space_constraint(args[place], pltpu.HBM)
    return pl.pallas_call(
        kernel,
        out_shape=outs if single else tuple(
            pltpu.HBM(out.shape, out.dtype) if n in hbm_out else out for n, out in enumerate(outs)
        ),
        in_specs=specs,
        out_specs=vmem if single else tuple(far if n in hbm_out else vmem for n in range(len(outs))),
        scratch_shapes=list(scratch),
        compiler_params=pltpu.CompilerParams(vmem_limit_bytes=50 * 2**20),
        name=name,
    )(*args)


def exchange(value, axes):
    return lax.all_to_all(value, axes, 0, 0, tiled=True)


def body(embeddings, frequencies, phases, solution, residual, direction):
    rows = whole((ROWS, LEAF))
    half = whole((HALF, HALF))
    leaf_points = pltpu.VMEM((LEAF, EMBED), bf16)
    leaf_rows = pltpu.VMEM((ROWS, LEAF), f32)
    block = pltpu.VMEM((HALF, HALF), f32)
    panel = pltpu.VMEM((LEVELS, LEAF, RANK), f32)
    feat, part_first, part = call(
        features_kernel,
        (whole((LEVELS, LEAF, RANK)), whole((ROWS, RANK)), whole((ROWS * 16, 128))),
        embeddings, frequencies, phases, direction,
        hbm=[(n, "hbm") for n in range(4)],
        hbm_out=(0,),
        scratch=(
            leaf_points,
            pltpu.VMEM((EMBED, RANK), bf16),
            pltpu.VMEM((LEVELS, RANK), f32),
            leaf_rows,
            pltpu.VMEM((LEAF, RANK), f32),
            panel,
            pltpu.VMEM((LEVELS, LEAF, RANK), bf16),
            pltpu.VMEM((LEVELS, LEAF, RANK), bf16),
            pltpu.SemaphoreType.DMA((5,)),
        ),
        name="features",
    )
    other_first = lax.ppermute(part_first, "z", [(n, n ^ 1) for n in range(8)])
    received = exchange(part.reshape(ROWS, 16, 128), ("x", "z"))
    near, matrix, largest = call(
        leaf_matrix_kernel, (rows, whole((LEAF, LEAF)), whole((8, 128))), embeddings, direction, part_first,
        hbm=[(0, "hbm"), (1, "hbm"), (2, "any")],
        scratch=(leaf_points, leaf_rows, pltpu.VMEM((LEAF, LEAF), f32), pltpu.SemaphoreType.DMA((2,))),
        name="leaf_matrix",
    )
    middle = call(
        middle_send_kernel, whole((GRP, 8, 128)), received, largest, other_first,
        hbm=[(1, "any"), (2, "any")], name="middle_send",
    )
    wide = exchange(middle, ("y", "c"))
    first, across, schur = call(
        leaf_first_kernel, (half, half, half), matrix, largest, middle, hbm=[(2, "any")], hbm_out=(0, 1),
        scratch=(block, block, pltpu.SemaphoreType.DMA((2,))), name="leaf_first",
    )
    place = lax.axis_index("y").astype(jnp.int32).reshape(1)
    back = call(
        middle_return_kernel, whole((PTS, 16, 128)), place, received, wide, schur,
        hbm=[(3, "any")], scalars=1, name="middle_return",
    )
    returned = exchange(back, ("x", "z"))
    solved, inv = call(
        leaf_second_kernel, (rows, whole((3, LEAF, LEAF), bf16)), first, across, schur, largest, matrix, residual, back,
        hbm=[(0, "hbm"), (1, "hbm"), (5, "hbm"), (6, "any")],
        scratch=(block, block, leaf_rows, pltpu.VMEM((LEAF, LEAF), f32), pltpu.SemaphoreType.DMA((3,))),
        name="leaf_second",
    )
    image, shifted, sums = call(
        image_kernel, (rows, rows, whole((1, 128))),
        part_first, other_first, returned.reshape(PTS * 16, 128), feat, near, direction, residual, solved, inv,
        hbm=[(3, "hbm"), (5, "hbm"), (6, "hbm")],
        scratch=(panel, leaf_rows, leaf_rows, pltpu.SemaphoreType.DMA((LEVELS + 2,))),
        name="image",
    )
    gathered = exchange(jnp.broadcast_to(sums[None], (GRP, 1, 128)), ("y", "c"))
    middle_sums = call(sum_spread_kernel, whole((PTS, 1, 128)), gathered, name="sum_spread")
    totals = exchange(middle_sums, ("x", "z"))
    return call(
        finish_kernel, (rows, rows, rows), totals, solution, residual, direction, solved, image, shifted, name="finish"
    )


def solution(mesh):
    torus = Mesh(mesh.devices.reshape(8, 2, 4, 8), AXES)
    columns = P(None, AXES)
    return jax.shard_map(
        body,
        mesh=torus,
        in_specs=(P(AXES, None), P(), P(), columns, columns, columns),
        out_specs=(columns, columns, columns),
        check_vma=False,
    )
```

```python
import math

import jax
import jax.numpy as jnp
import numpy as np
from jax import lax
from jax.experimental import pallas as pl
from jax.experimental.pallas import tpu as pltpu
from jax.sharding import Mesh
from jax.sharding import PartitionSpec as P

AXES = ("y", "c", "x", "z")
LEAF, EMBED, RANK, ROWS, LEVELS = 512, 768, 256, 32, 9
PTS, GRP = 32, 16
RIDGE = 0.5
HALF = LEAF // 2
CHUNK = 32

f32 = jnp.float32
bf16 = jnp.bfloat16
highest = lax.Precision.HIGHEST


SINE_DEGREE = 4
PEAK = math.sqrt(2.0 / RANK)


def sine_coefficients():
    cheb = np.polynomial.chebyshev
    nodes = np.cos(np.pi * (np.arange(64) + 0.5) / 64)
    part = np.sqrt((nodes + 1.0) / 8.0)
    series = cheb.chebfit(nodes, np.sin(np.pi * part) / part, SINE_DEGREE)
    poly = np.polynomial.Polynomial(cheb.cheb2poly(series))
    shifted = poly(np.polynomial.Polynomial([-1.0, 8.0]))
    return [float(value) for value in shifted.coef * math.sqrt(2.0 * PEAK)]


SINE = sine_coefficients()
TURN = 2.0 * math.pi


def scaled_cosine(turns):
    part = turns - jnp.round(turns)
    square = part * part
    value = SINE[-1] * square + SINE[-2]
    for coefficient in SINE[-3::-1]:
        value = value * square + coefficient
    sine = value * part
    return PEAK - sine * sine


def split(value):
    high = value.astype(bf16)
    return high, (value - high.astype(f32)).astype(bf16)


def mm(left, right):
    return jnp.dot(left, right, preferred_element_type=f32)


def mm_t(left, right, precision=None):
    return lax.dot_general(
        left, right, (((1,), (1,)), ((), ())), preferred_element_type=f32, precision=precision
    )


def mm3(left, right):
    return mm(left[0], right[0]) + (mm(left[0], right[1]) + mm(left[1], right[0]))


def planes(value):
    high = value.astype(bf16)
    rest = value - high.astype(f32)
    middle = rest.astype(bf16)
    return high, middle, (rest - middle.astype(f32)).astype(bf16)


def six_products(left, right, product):
    rows = left[0].shape[0]
    first = product(jnp.concatenate(left, axis=0), right[0])
    second = product(jnp.concatenate(left[:2], axis=0), right[1])
    third = product(left[0], right[2])
    small = third + second[rows:] + first[2 * rows :]
    return first[:rows] + ((first[rows : 2 * rows] + second[:rows]) + small)


def mm6(left, right):
    return jnp.dot(left, right, preferred_element_type=f32, precision=highest)


def length_scale(depth):
    return 0.5 * 2.0 ** (depth / 8.0)


def features_kernel(
    emb_in, freq_in, phase_in, direction_in, feat, part_first, part,
    emb, freq, phase, direction, proj, keep, high, low, sems,
):
    loads = [
        pltpu.make_async_copy(source, target, sems.at[n])
        for n, (source, target) in enumerate(
            ((emb_in, emb), (freq_in, freq), (phase_in, phase), (direction_in, direction))
        )
    ]
    for load in loads:
        load.start()
    for load in loads[:2]:
        load.wait()
    proj[...] = mm(emb[...], freq[...])
    for load in loads[2:]:
        load.wait()
    phase_turns = phase[...] * (1.0 / TURN)

    def chunk(step, carry):
        rows = pl.ds(pl.multiple_of(step * CHUNK, CHUNK), CHUNK)
        block = proj[rows, :]
        for level in range(LEVELS):
            turns = block * (1.0 / (TURN * length_scale(level + 1))) + phase_turns[level : level + 1, :]
            value = scaled_cosine(turns)
            keep[level, rows, :] = value
            high_part, low_part = split(value)
            high[level, rows, :] = high_part
            low[level, rows, :] = low_part
        pltpu.make_async_copy(keep.at[:, rows, :], feat.at[:, rows, :], sems.at[4]).start()
        return carry

    lax.fori_loop(0, LEAF // CHUNK, chunk, 0)
    direction_high, direction_low = split(direction[...])
    stacked = jnp.concatenate([direction_high, direction_low], axis=0)
    for level in range(LEVELS):
        both = mm(stacked, high[level])
        total = both[:ROWS] + (both[ROWS:] + mm(direction_high, low[level]))
        if level == 0:
            part_first[...] = total
        else:
            slot = 2 * (level - 1)
            part[pl.ds(slot, ROWS, stride=16), :] = total[:, :128]
            part[pl.ds(slot + 1, ROWS, stride=16), :] = total[:, 128:]
    pltpu.make_async_copy(keep, feat, sems.at[4]).wait()


def eye_block():
    row = lax.broadcasted_iota(jnp.int32, (HALF, HALF), 0)
    column = lax.broadcasted_iota(jnp.int32, (HALF, HALF), 1)
    return jnp.where(row == column, 1.0, 0.0).astype(f32)


def inverse_block(block, largest):
    eye = eye_block()
    start = 2.0 / (RIDGE + largest)
    scale = jnp.minimum((largest + RIDGE) / jnp.maximum(largest - RIDGE, 1e-3), 1e4)
    error = eye - start * block
    inverse = None
    for step in range(7):
        double = 2.0 * scale * scale
        gain = double / (double - 1.0)
        error_parts = split(error)
        if step == 0:
            inverse = (gain * start) * (eye + error)
        else:
            inverse = gain * (inverse + mm3(split(inverse), error_parts))
        if step < 6:
            error = gain * mm3(error_parts, error_parts) - (gain / double) * eye
            scale = jnp.minimum(double - 1.0, 1e4)
    error = eye - mm6(block, inverse)
    inverse = inverse + mm3(split(inverse), split(error))
    return inverse


def leaf_matrix_kernel(
    emb_in, direction_in, after, near, matrix, largest_out, emb, direction, grid, sems
):
    loads = [
        pltpu.make_async_copy(emb_in, emb, sems.at[0]),
        pltpu.make_async_copy(direction_in, direction, sems.at[1]),
    ]
    for load in loads:
        load.start()
    for load in loads:
        load.wait()
    points = emb[...]
    wide = points.astype(f32)
    square_high, square_low = split(wide * wide)
    ones_left = jnp.ones((8, EMBED), bf16)
    ones_right = jnp.ones((EMBED, 128), bf16)
    along = (mm_t(ones_left, square_high) + mm_t(ones_left, square_low))[:1, :]
    down = (mm(square_high, ones_right) + mm(square_low, ones_right))[:, :1]
    grid[...] = down + along
    matrix[...] = mm_t(points, points)

    def chunk(step, carry):
        begin = pl.multiple_of(step * CHUNK, CHUNK)
        rows = pl.ds(begin, CHUNK)
        distances = grid[rows, :] - 2.0 * matrix[rows, :]
        value = math.sqrt(RANK / LEAF) * jnp.exp(distances * (-1.0 / 0.5))
        row = begin + lax.broadcasted_iota(jnp.int32, (CHUNK, LEAF), 0)
        column = lax.broadcasted_iota(jnp.int32, (CHUNK, LEAF), 1)
        matrix[rows, :] = value + jnp.where(row == column, RIDGE, 0.0)
        return carry

    lax.fori_loop(0, LEAF // CHUNK, chunk, 0)
    near[...] = six_products(planes(direction[...]), planes(matrix[...]), mm)
    sums = jnp.sum(matrix[...], axis=0, keepdims=True)
    largest = jnp.max(sums, axis=1, keepdims=True)
    largest_out[...] = jnp.broadcast_to(largest, (8, 128))


def leaf_first_kernel(matrix, largest, after, first_out, across_out, schur_out, first_keep, across_keep, sems):
    side = matrix[:HALF, HALF:]
    first = inverse_block(matrix[:HALF, :HALF], largest[:1, :1])
    first_keep[...] = first
    across = mm6(first, side)
    across_keep[...] = across
    stores = [
        pltpu.make_async_copy(first_keep, first_out, sems.at[0]),
        pltpu.make_async_copy(across_keep, across_out, sems.at[1]),
    ]
    for store in stores:
        store.start()
    schur_out[...] = matrix[HALF:, HALF:] - mm6(jnp.transpose(across), side)
    for store in stores:
        store.wait()


def leaf_second_kernel(
    first_in, across_in, schur, largest, matrix, residual_in, after, solved, inv,
    first, across_scratch, residual, whole_inverse, sems,
):
    loads = [
        pltpu.make_async_copy(source, target, sems.at[n])
        for n, (source, target) in enumerate(
            ((first_in, first), (across_in, across_scratch), (residual_in, residual))
        )
    ]
    for load in loads:
        load.start()
    second = inverse_block(schur[...], largest[:1, :1])
    for load in loads:
        load.wait()
    across = across_scratch[...]
    lower = -mm6(second, jnp.transpose(across))
    top = first[...] - mm6(across, lower)
    whole_inverse[:HALF, :HALF] = top
    whole_inverse[HALF:, :HALF] = lower
    whole_inverse[:HALF, HALF:] = jnp.transpose(lower)
    whole_inverse[HALF:, HALF:] = second
    row = lax.broadcasted_iota(jnp.int32, (LEAF, LEAF), 0)
    column = lax.broadcasted_iota(jnp.int32, (LEAF, LEAF), 1)
    start = whole_inverse[...]
    start_planes = planes(start)
    error = jnp.where(row == column, 1.0, 0.0) - six_products(planes(matrix[...]), start_planes, mm)
    error_high = error.astype(bf16)
    better = start + (mm(start_planes[0], error_high) + mm(start_planes[1], error_high))
    for n, plane in enumerate(planes(better)):
        inv[n] = plane
    solved[...] = six_products(planes(residual[...]), [inv[n] for n in range(3)], mm)


def middle_send_kernel(received, first_after, second_after, out):
    total = received[0, 8:16, :]
    for source in range(1, PTS):
        total = total + received[source, 8:16, :]
    for target in range(GRP):
        out[target] = total


def row_select(tiles):
    row = lax.broadcasted_iota(jnp.int32, (8, 128), 0)
    return jnp.where(row < 2, tiles[0], jnp.where(row < 4, tiles[1], jnp.where(row < 6, tiles[2], tiles[3])))


def middle_return_kernel(place, received, wide, after, out):
    sums = [received[source, 0:8, :] for source in range(PTS)]
    stages = []
    for _ in range(5):
        sums = [sums[2 * n] + sums[2 * n + 1] for n in range(len(sums) // 2)]
        stages.append(sums)
    line = place[0]
    upper = []
    for depth in range(4):
        base = (line >> depth) << (depth + 1)
        total = wide[base] + wide[base + 1]
        for source in range(2, 2 ** (depth + 1)):
            total = total + wide[base + source]
        upper.append(total)
    top = row_select(upper)
    for node in range(8):
        low = row_select([stages[1][node], stages[2][node // 2], stages[3][node // 4], stages[4][0]])
        for leaf in range(4):
            out[node * 4 + leaf, 0:8, :] = low
            out[node * 4 + leaf, 8:16, :] = top


def image_kernel(
    own_first, other_first, returned, feat_in, near, direction_in, residual_in, solved, inv, image, shifted, out,
    feat, direction, residual, sems,
):
    loads = [pltpu.make_async_copy(feat_in.at[n], feat.at[n], sems.at[n]) for n in range(LEVELS)]
    loads.append(pltpu.make_async_copy(direction_in, direction, sems.at[LEVELS]))
    loads.append(pltpu.make_async_copy(residual_in, residual, sems.at[LEVELS + 1]))
    for load in loads:
        load.start()
    spread = near[...]
    for level in range(LEVELS):
        if level == 0:
            total = own_first[...] + other_first[...]
        else:
            slot = 2 * (level - 1)
            total = jnp.concatenate(
                [returned[pl.ds(slot, ROWS, stride=16), :], returned[pl.ds(slot + 1, ROWS, stride=16), :]],
                axis=1,
            )
        weight = math.sqrt(RANK / (LEAF * 2 ** (level + 1)))
        loads[level].wait()
        spread = spread + six_products(planes(total * weight), planes(feat[level]), mm_t)
    image[...] = spread
    moved = six_products(planes(spread), [inv[n] for n in range(3)], mm)
    shifted[...] = moved
    loads[LEVELS].wait()
    loads[LEVELS + 1].wait()
    first = solved[...]
    products = jnp.concatenate(
        [residual[...] * first, direction[...] * spread, first * spread, spread * moved], axis=0
    )
    folded = products[:, :128] + products[:, 128:256] + (products[:, 256:384] + products[:, 384:])
    out[...] = jnp.sum(jnp.transpose(folded), axis=0, keepdims=True)


def sum_spread_kernel(received, out):
    total = received[0]
    for source in range(1, GRP):
        total = total + received[source]
    for target in range(PTS):
        out[target] = total


def finish_kernel(received, solution, residual, direction, solved, image, shifted, new_solution, new_residual, new_direction):
    total = received[0]
    for source in range(1, PTS):
        total = total + received[source]
    row = lax.broadcasted_iota(jnp.int32, (ROWS, 128), 0)
    column = lax.broadcasted_iota(jnp.int32, (ROWS, 128), 1)
    spread = jnp.broadcast_to(total, (ROWS, 128))

    def pick(slot):
        return jnp.sum(jnp.where(column == row + ROWS * slot, spread, 0.0), axis=1, keepdims=True)

    norm_old, curvature, cross, moved = pick(0), pick(1), pick(2), pick(3)
    step = norm_old / curvature
    norm_new = norm_old - step * (2.0 * cross - step * moved)
    ratio = norm_new / norm_old
    direction_value = direction[...]
    new_solution[...] = solution[...] + step * direction_value
    new_residual[...] = residual[...] - step * image[...]
    new_direction[...] = (solved[...] - step * shifted[...]) + ratio * direction_value


def whole(shape, dtype=f32):
    return jax.ShapeDtypeStruct(shape, dtype)


def call(kernel, outs, *args, scratch=(), name=None, hbm=(), scalars=0, hbm_out=()):
    vmem = pl.BlockSpec(memory_space=pltpu.VMEM)
    smem = pl.BlockSpec(memory_space=pltpu.SMEM)
    far = pl.BlockSpec(memory_space=pltpu.HBM)
    anywhere = pl.BlockSpec(memory_space=pl.ANY)
    single = not isinstance(outs, (tuple, list))
    kinds = {"hbm": far, "any": anywhere}
    specs = [smem if n < scalars else vmem for n in range(len(args))]
    args = list(args)
    for place, kind in hbm:
        specs[place] = kinds[kind]
        if kind == "hbm":
            args[place] = pltpu.with_memory_space_constraint(args[place], pltpu.HBM)
    return pl.pallas_call(
        kernel,
        out_shape=outs if single else tuple(
            pltpu.HBM(out.shape, out.dtype) if n in hbm_out else out for n, out in enumerate(outs)
        ),
        in_specs=specs,
        out_specs=vmem if single else tuple(far if n in hbm_out else vmem for n in range(len(outs))),
        scratch_shapes=list(scratch),
        compiler_params=pltpu.CompilerParams(vmem_limit_bytes=50 * 2**20),
        name=name,
    )(*args)


def exchange(value, axes):
    return lax.all_to_all(value, axes, 0, 0, tiled=True)


def body(embeddings, frequencies, phases, solution, residual, direction):
    rows = whole((ROWS, LEAF))
    half = whole((HALF, HALF))
    leaf_points = pltpu.VMEM((LEAF, EMBED), bf16)
    leaf_rows = pltpu.VMEM((ROWS, LEAF), f32)
    block = pltpu.VMEM((HALF, HALF), f32)
    panel = pltpu.VMEM((LEVELS, LEAF, RANK), f32)
    feat, part_first, part = call(
        features_kernel,
        (whole((LEVELS, LEAF, RANK)), whole((ROWS, RANK)), whole((ROWS * 16, 128))),
        embeddings, frequencies, phases, direction,
        hbm=[(n, "hbm") for n in range(4)],
        hbm_out=(0,),
        scratch=(
            leaf_points,
            pltpu.VMEM((EMBED, RANK), bf16),
            pltpu.VMEM((LEVELS, RANK), f32),
            leaf_rows,
            pltpu.VMEM((LEAF, RANK), f32),
            panel,
            pltpu.VMEM((LEVELS, LEAF, RANK), bf16),
            pltpu.VMEM((LEVELS, LEAF, RANK), bf16),
            pltpu.SemaphoreType.DMA((5,)),
        ),
        name="features",
    )
    other_first = lax.ppermute(part_first, "z", [(n, n ^ 1) for n in range(8)])
    received = exchange(part.reshape(ROWS, 16, 128), ("x", "z"))
    near, matrix, largest = call(
        leaf_matrix_kernel, (rows, whole((LEAF, LEAF)), whole((8, 128))), embeddings, direction, part_first,
        hbm=[(0, "hbm"), (1, "hbm"), (2, "any")],
        scratch=(leaf_points, leaf_rows, pltpu.VMEM((LEAF, LEAF), f32), pltpu.SemaphoreType.DMA((2,))),
        name="leaf_matrix",
    )
    middle = call(
        middle_send_kernel, whole((GRP, 8, 128)), received, largest, other_first,
        hbm=[(1, "any"), (2, "any")], name="middle_send",
    )
    wide = exchange(middle, ("y", "c"))
    first, across, schur = call(
        leaf_first_kernel, (half, half, half), matrix, largest, middle, hbm=[(2, "any")], hbm_out=(0, 1),
        scratch=(block, block, pltpu.SemaphoreType.DMA((2,))), name="leaf_first",
    )
    place = lax.axis_index("y").astype(jnp.int32).reshape(1)
    back = call(
        middle_return_kernel, whole((PTS, 16, 128)), place, received, wide, schur,
        hbm=[(3, "any")], scalars=1, name="middle_return",
    )
    returned = exchange(back, ("x", "z"))
    solved, inv = call(
        leaf_second_kernel, (rows, whole((3, LEAF, LEAF), bf16)), first, across, schur, largest, matrix, residual, back,
        hbm=[(0, "hbm"), (1, "hbm"), (5, "hbm"), (6, "any")],
        scratch=(block, block, leaf_rows, pltpu.VMEM((LEAF, LEAF), f32), pltpu.SemaphoreType.DMA((3,))),
        name="leaf_second",
    )
    image, shifted, sums = call(
        image_kernel, (rows, rows, whole((1, 128))),
        part_first, other_first, returned.reshape(PTS * 16, 128), feat, near, direction, residual, solved, inv,
        hbm=[(3, "hbm"), (5, "hbm"), (6, "hbm")],
        scratch=(panel, leaf_rows, leaf_rows, pltpu.SemaphoreType.DMA((LEVELS + 2,))),
        name="image",
    )
    gathered = exchange(jnp.broadcast_to(sums[None], (GRP, 1, 128)), ("y", "c"))
    middle_sums = call(sum_spread_kernel, whole((PTS, 1, 128)), gathered, name="sum_spread")
    totals = exchange(middle_sums, ("x", "z"))
    return call(
        finish_kernel, (rows, rows, rows), totals, solution, residual, direction, solved, image, shifted, name="finish"
    )


def solution(mesh):
    torus = Mesh(mesh.devices.reshape(8, 2, 4, 8), AXES)
    columns = P(None, AXES)
    return jax.shard_map(
        body,
        mesh=torus,
        in_specs=(P(AXES, None), P(), P(), columns, columns, columns),
        out_specs=(columns, columns, columns),
        check_vma=False,
    )
```
